512 devices in a mesh: seq: 64 (over z_hi, y, core), tp: 8 (over x, z_lo).
Axes of the slice: x: 4, y: 8, z: 8 (z_hi: 4, z_lo: 2; z = z_hi * 2 + z_lo), core: 2. Of those that a mesh axis runs over, the one named last changes fastest.
Arguments:
- prompt_states: bfloat16 [2, 64, 64, 2048], P(None, 'seq', None, 'tp'), may hold values from -8 to 8
- cont_states: bfloat16 [2, 64, 8, 2048], P(None, 'seq', None, 'tp'), may hold values from -8 to 8
- cache_kv: bfloat16 [2, 64, 448, 2048], P(None, 'seq', None, 'tp'), may hold values from -5 to 5
- cache_lengths: int32 [64], replicated, may hold values from 1 to 448, 14336 in all
- w_query: bfloat16 [2048, 2048], P(None, 'tp'), may hold values from -2 to 2
- w_key: bfloat16 [2048, 2048], P(None, 'tp'), may hold values from -2 to 2
- w_value: bfloat16 [2048, 2048], P(None, 'tp'), may hold values from -0.125 to 0.125
- w_out: bfloat16 [2048, 2048], P('tp'), may hold values from -2 to 2
- q_gain: float32 [2048], P('tp'), may hold values from 0 to 10
- k_gain: float32 [2048], P('tp'), may hold values from 0 to 10
- post_gain: float32 [2048], P('tp'), may hold values from 0.5 to 1.5
Outputs:
- hidden_prompt: bfloat16 [2, 64, 64, 2048], P(None, 'seq', None, 'tp')
- hidden_cont: bfloat16 [2, 64, 8, 2048], P(None, 'seq', None, 'tp')
- kv_cache: bfloat16 [2, 64, 128, 2048], P(None, 'seq', None, 'tp')
The draws below stay inside these ranges and needn't reach their ends.
Inputs may be any that keep to these rules, and one draw needn't show every extreme that they name: The cache_lengths[d] live slots of seq index d are its first ones; the lengths sum to 14336 and the largest equals 448.
All inputs are finite; a program needn't handle non-finite values.
Results may differ from the reference program's by a relative error of at most 0.029.
Values may be sent and summed in bfloat16 or wider, within the bound.
A program may use at most 64 MiB of HBM per device.

```python
import math
import jax
import jax.numpy as jnp
import numpy as np
from jax import lax

D = 2048
H = 16
HD = 128
BLK = 64
CBLK = 8
CACHE_DEV = 448
PROMPT = 8192
CONT = 1024
CACHED = 14336
N_SEQ = 64


def row_scaled(key, shape):
    noise_key, scale_key = jax.random.split(key)
    scale_shape = shape[:-1] + (1,)
    raw_noise = jnp.clip(jax.random.normal(noise_key, shape, jnp.float32), -4.0, 4.0)
    row_scale = jnp.exp(jax.random.uniform(scale_key, scale_shape, jnp.float32, math.log(0.5), math.log(2.0)))
    return raw_noise * row_scale


def rising_weight(key, row_count, col_count, fan_width):
    raw_noise = jnp.clip(jax.random.normal(key, (row_count, col_count), jnp.float32), -4.0, 4.0)
    column = jnp.arange(col_count, dtype=jnp.float32) / (col_count - 1) - 0.5
    column_rise = 3.0 ** column
    return raw_noise * column_rise[None, :] / math.sqrt(fan_width)


def head_gain(key):
    head_key, noise_key = jax.random.split(key)
    factor = jnp.exp(jax.random.uniform(head_key, (H, 1), jnp.float32, math.log(0.7), math.log(1.4)))
    jitter = 1.0 + 0.2 * jax.random.uniform(noise_key, (H, HD), jnp.float32, -1.0, 1.0)
    return (factor * jitter).reshape(H * HD)


def draw_prompt_states(key, part):
    return row_scaled(jax.random.fold_in(key, 11), (2, N_SEQ, BLK, D)).astype(jnp.bfloat16)


def draw_cont_states(key, part):
    return row_scaled(jax.random.fold_in(key, 12), (2, N_SEQ, CBLK, D)).astype(jnp.bfloat16)


def draw_w_query(key, part):
    return rising_weight(jax.random.fold_in(key, 21), D, H * HD, D).astype(jnp.bfloat16)


def draw_w_key(key, part):
    return rising_weight(jax.random.fold_in(key, 22), D, H * HD, D).astype(jnp.bfloat16)


def draw_w_out(key, part):
    return rising_weight(jax.random.fold_in(key, 23), H * HD, D, H * HD).astype(jnp.bfloat16)


def draw_q_gain(key, part):
    return head_gain(jax.random.fold_in(key, 31))


def draw_k_gain(key, part):
    return head_gain(jax.random.fold_in(key, 32))


def block_levels(key, extent, shards, low, high):
    level = 1.0
    for dim, blocks in shards:
        heights = jax.random.uniform(jax.random.fold_in(jax.random.fold_in(key, 6), dim), (blocks,), jnp.float32, low / len(shards), high / len(shards))
        level = level * jnp.repeat(jnp.exp(heights), extent[dim] // blocks).reshape((-1,) + (1,) * (len(extent) - 1 - dim))
    return level


def profile(number_of, total, limit, slope):
    loads = [(1 << 20) // math.isqrt(rank ** slope) + 1 for rank in range(2, number_of + 1)]
    spare, given = total - limit - (number_of - 1), [1] * (number_of - 1)
    while spare > 0:
        candidates = [i for i in range(number_of - 1) if given[i] < limit]
        pool, left = sum([loads[i] for i in candidates]), spare
        for i in candidates:
            addition = min(limit - given[i], max(1, left * loads[i] // pool), spare)
            given[i] = given[i] + addition
            spare = spare - addition
    return np.array([limit] + given)


def ragged_sizes(rng, count, total, most, lean):
    if count == 2:
        one = jax.random.randint(rng, (), max(1, total - most), min(most, total - 1) + 1)
        return jnp.stack([one, total - one])
    tallies = jnp.asarray(profile(count, total, most, lean), jnp.int32)
    pairs = (count - 1) // 2
    source_of, receiver = tallies[1:1 + 2 * pairs:2], tallies[2:2 + 2 * pairs:2]
    room = jnp.minimum(source_of - 1, most - receiver)
    passed = jax.random.randint(jax.random.fold_in(rng, 1), (pairs,), 0, 1 << 20) % (room + 1)
    tallies = tallies.at[1:1 + 2 * pairs:2].set(source_of - passed).at[2:2 + 2 * pairs:2].set(receiver + passed)
    return tallies[jax.random.permutation(jax.random.fold_in(rng, 2), count)]


def bell_draw(rng, dims, spread, limit, shards=(), kind=jnp.bfloat16):
    drawn = jax.random.normal(rng, dims, jnp.float32) * spread
    if len(shards) > 0:
        drawn = block_levels(rng, dims, shards, -0.22, 0.18) * drawn
    return jnp.clip(drawn, min=-limit, max=limit).astype(kind)


def setup_inputs(seed: int = 0) -> dict:
    arg_keys = jax.random.split(jax.random.key(seed), 12)
    prompt_states = draw_prompt_states(jax.random.fold_in(arg_keys[11], 71), 0)
    cont_states = draw_cont_states(jax.random.fold_in(arg_keys[11], 71), 0)
    cache_kv = bell_draw(arg_keys[2], (2, N_SEQ, CACHE_DEV, H * HD), 1.0, 5.0, ((1, 64), (3, 8)))
    cache_lengths = ragged_sizes(arg_keys[3], N_SEQ, CACHED, CACHE_DEV, 2).astype(jnp.int32)
    w_query = draw_w_query(jax.random.fold_in(arg_keys[11], 71), 0)
    w_key = draw_w_key(jax.random.fold_in(arg_keys[11], 71), 0)
    w_value = bell_draw(arg_keys[6], (D, H * HD), D ** -0.5, 0.125, ((1, 8),))
    w_out = draw_w_out(jax.random.fold_in(arg_keys[11], 71), 0)
    q_gain = draw_q_gain(jax.random.fold_in(arg_keys[11], 71), 0)
    k_gain = draw_k_gain(jax.random.fold_in(arg_keys[11], 71), 0)
    post_gain = jnp.clip(1.0 + 0.1 * jax.random.normal(arg_keys[10], (D,), jnp.float32), 0.5, 1.5)
    return {"prompt_states": prompt_states, "cont_states": cont_states, "cache_kv": cache_kv, "cache_lengths": cache_lengths, "w_query": w_query, "w_key": w_key, "w_value": w_value, "w_out": w_out, "q_gain": q_gain, "k_gain": k_gain, "post_gain": post_gain}


EPS = 1e-06
THETA = 500000.0
NEG = -1e+30

def rotate(field, positions):
    half_dim = field.shape[-1] // 2
    inverse = THETA ** (-(jnp.arange(half_dim, dtype=jnp.float32) * 2.0 / field.shape[-1]))
    angles = positions.astype(jnp.float32)[:, None] * inverse[None, :]
    cosine = jnp.cos(angles)[:, None, :]
    sine_part = jnp.sin(angles)[:, None, :]
    front_half = field[..., :half_dim]
    back_half = field[..., half_dim:]
    return jnp.concatenate([front_half * cosine - back_half * sine_part, back_half * cosine + front_half * sine_part], -1)

def rms_scale(field, gain):
    mean_sq = lax.optimization_barrier(jnp.mean(field * field, -1, keepdims=True))
    return field * lax.rsqrt(mean_sq + EPS) * gain.astype(jnp.float32)[None, :]

def attend_head(queries, keys, values, allowed):
    scores = jnp.dot(queries, keys.T, preferred_element_type=jnp.float32) * HD ** (-0.5)
    scores = jnp.where(allowed, scores, NEG)
    row_max = lax.optimization_barrier(jnp.max(scores, -1, keepdims=True))
    weights = jnp.where(allowed, jnp.exp(scores - row_max), 0.0)
    summed = jnp.dot(weights.astype(jnp.bfloat16), values, preferred_element_type=jnp.float32)
    return summed / lax.optimization_barrier(jnp.sum(weights, -1, keepdims=True))

def by_heads(queries, keys, values, allowed):

    def one_head(triple):
        return attend_head(triple[0], triple[1], triple[2], allowed)
    result = lax.map(one_head, (queries.transpose(1, 0, 2), keys.transpose(1, 0, 2), values.transpose(1, 0, 2)))
    return result.transpose(1, 0, 2).reshape(queries.shape[0], H * HD)

def reference(prompt_states, cont_states, cache_kv, cache_lengths, w_query, w_key, w_value, w_out, q_gain, k_gain, post_gain):
    seq_prompt = jnp.concatenate([prompt_states[0], prompt_states[1][::-1]], 0).reshape(PROMPT, D)
    seq_cont = jnp.concatenate([cont_states[0], cont_states[1][::-1]], 0).reshape(CONT, D)
    all_rows = jnp.concatenate([seq_prompt, seq_cont], 0)
    query_proj = jnp.dot(all_rows, w_query, preferred_element_type=jnp.float32)
    key_proj = jnp.dot(all_rows, w_key, preferred_element_type=jnp.float32)
    value_proj = jnp.dot(all_rows, w_value, preferred_element_type=jnp.float32)
    values = value_proj.astype(jnp.bfloat16).reshape(-1, H, HD)
    positions = jnp.concatenate([jnp.arange(PROMPT, dtype=jnp.int32), CACHED + jnp.arange(CONT, dtype=jnp.int32)])
    queries = rotate(rms_scale(query_proj, q_gain).reshape(-1, H, HD), positions).astype(jnp.bfloat16)
    keys = rotate(rms_scale(key_proj, k_gain).reshape(-1, H, HD), positions).astype(jnp.bfloat16)
    pieces_out = []
    prompt_block = PROMPT // 8
    for block_index in range(8):
        low_row = block_index * prompt_block
        high_row = low_row + prompt_block
        query_pos = jnp.arange(low_row, high_row, dtype=jnp.int32)
        key_pos = jnp.arange(high_row, dtype=jnp.int32)
        allowed = key_pos[None, :] <= query_pos[:, None]
        pieces_out.append(by_heads(queries[low_row:high_row], keys[:high_row], values[:high_row], allowed))
    cache_keys = cache_kv[0].reshape(N_SEQ * CACHE_DEV, H, HD)
    cache_values = cache_kv[1].reshape(N_SEQ * CACHE_DEV, H, HD)
    live_slots = (jnp.arange(CACHE_DEV, dtype=jnp.int32)[None, :] < cache_lengths[:, None]).reshape(-1)
    cont_keys = jnp.concatenate([cache_keys, keys[PROMPT:]], 0)
    cont_values = jnp.concatenate([cache_values, values[PROMPT:]], 0)
    cont_block = CONT // 4
    for block_index in range(4):
        low_row = block_index * cont_block
        high_row = low_row + cont_block
        query_pos = jnp.arange(low_row, high_row, dtype=jnp.int32)
        new_allowed = jnp.arange(CONT, dtype=jnp.int32)[None, :] <= query_pos[:, None]
        cache_allowed = jnp.broadcast_to(live_slots[None, :], (cont_block, N_SEQ * CACHE_DEV))
        allowed = jnp.concatenate([cache_allowed, new_allowed], 1)
        pieces_out.append(by_heads(queries[PROMPT + low_row:PROMPT + high_row], cont_keys, cont_values, allowed))
    attended = jnp.concatenate(pieces_out, 0).astype(jnp.bfloat16)
    projected = jnp.dot(attended, w_out, preferred_element_type=jnp.float32)
    hidden = (all_rows.astype(jnp.float32) + rms_scale(projected, post_gain)).astype(jnp.bfloat16)
    hidden_seq = hidden[:PROMPT].reshape(2 * N_SEQ, BLK, D)
    hidden_prompt = jnp.stack([hidden_seq[:N_SEQ], hidden_seq[N_SEQ:][::-1]])
    cont_seq = hidden[PROMPT:].reshape(2 * N_SEQ, CBLK, D)
    hidden_cont = jnp.stack([cont_seq[:N_SEQ], cont_seq[N_SEQ:][::-1]])
    stacked = jnp.stack([keys[:PROMPT].reshape(PROMPT, H * HD), values[:PROMPT].reshape(PROMPT, H * HD)])
    kv_cache = stacked.reshape(2, 2 * BLK, N_SEQ, H * HD).transpose(0, 2, 1, 3)
    return (hidden_prompt, hidden_cont, kv_cache)
```

```python
import math
import jax
import jax.numpy as jnp
import numpy as np
from jax import lax
from jax.experimental import pallas as pl
from jax.experimental.pallas import tpu as pltpu
from jax.sharding import PartitionSpec as P

HD = 128
EPS = 1e-06
THETA = 500000.0
NEG = -1e30
ZN, YN, CN, TP = 4, 8, 2, 8
CHIPS = ZN * YN
BLK, CBLK, CAP = 64, 8, 448
ROWS = 2 * BLK
CROWS = 2 * CBLK
ALL = ROWS + CROWS
W = 256
D = 2048
CACHED = 14336
KEYS = YN * CN * BLK
CKEYS = 1024
MSG = W + 128
QSCALE = math.log2(math.e) / math.sqrt(HD)
F32, BF16 = jnp.float32, jnp.bfloat16


def iota(shape, dim):
    return lax.broadcasted_iota(jnp.int32, shape, dim)


def attend(q, k, v, allowed):
    s = lax.dot_general(q, k, (((1,), (1,)), ((), ())), preferred_element_type=F32)
    s = jnp.where(allowed, s, NEG)
    m = jnp.max(s, -1, keepdims=True).astype(BF16).astype(F32)
    p = jnp.exp2(s - jnp.maximum(m, -1e29))
    total = jnp.sum(p, -1, keepdims=True)
    out = jnp.dot(p.astype(BF16), v, preferred_element_type=F32)
    return out, m, total


def message(parts):
    rows = parts[0][0].shape[0]
    lane = iota((rows, 128), 1)
    stats = jnp.zeros((rows, 128), F32)
    for h, (_, m, total) in enumerate(parts):
        high = total.astype(BF16).astype(F32)
        stats = jnp.where(lane == 3 * h, m, stats)
        stats = jnp.where(lane == 3 * h + 1, high, stats)
        stats = jnp.where(lane == 3 * h + 2, total - high, stats)
    return jnp.concatenate([p[0].astype(BF16) for p in parts] + [stats.astype(BF16)], -1)


def combine(pieces):
    outs = []
    stats = [p[:, W:].astype(F32) for p in pieces]
    for h in range(2):
        ms = [s[:, 3 * h : 3 * h + 1] for s in stats]
        ls = [s[:, 3 * h + 1 : 3 * h + 2] + s[:, 3 * h + 2 : 3 * h + 3] for s in stats]
        top = ms[0]
        for m in ms[1:]:
            top = jnp.maximum(top, m)
        num, den = 0.0, 0.0
        for p, m, l in zip(pieces, ms, ls):
            w = jnp.exp2(m - top)
            num = num + w * p[:, h * HD : (h + 1) * HD].astype(F32)
            den = den + w * l
        outs.append(num / den)
    return jnp.concatenate(outs, -1).astype(BF16)


def kernel(
    prompt, cont, cache, lengths, wq_h, wk_h, wv_h, wo_h, qgain, kgain, pgain, inv,
    hid_p, hid_c, kv_out,
    wq, wk, wv, wo, xg, xc, cos, sin, sq_out, sq_in, qg, kvg, qcg, kcc,
    oc_out, oc_in, op_out, op_in, kv_s, kv_r, att, pr_out, pr_in,
    local, tp_ss, tp_rs, tpc_ss, tpc_rs, sq_ss, sq_rs, core_ss, core_rs,
    qc_ss, qc_rs, q_ss, q_rs, ring_ss, ring_rs, pair_ss, pair_rs,
    oc_ss, oc_rs, op_ss, op_rs, kv_ss, kv_rs, pr_ss, pr_rs,
):
    s_idx = lax.axis_index("seq")
    t = lax.axis_index("tp")
    z = s_idx // (YN * CN)
    y = (s_idx // CN) % YN
    c = s_idx % CN
    chip = s_idx // CN
    x, zl = t // 2, t % 2

    def seq_of(z_, y_, c_):
        return (z_ * YN + y_) * CN + c_

    def remote(src, dst, ss, rs, seq=None, tp=None):
        dev = {"seq": s_idx if seq is None else seq, "tp": t if tp is None else tp}
        return pltpu.make_async_remote_copy(
            src_ref=src, dst_ref=dst, send_sem=ss, recv_sem=rs,
            device_id=dev, device_id_type=pl.DeviceIdType.MESH,
        )

    partner = s_idx + 1 - 2 * c
    hops = [(0, 1), (1, 0), (3, 0), (1, 1), (3, 1), (2, 0), (2, 1)]
    peers = [((x + dx) % 4) * 2 + (zl + dz) % 2 for dx, dz in hops]

    loads = [
        pltpu.make_async_copy(prompt, xg.at[t], local.at[0]),
        pltpu.make_async_copy(cont, xc.at[t], local.at[1]),
        pltpu.make_async_copy(wq_h, wq, local.at[2]),
        pltpu.make_async_copy(wk_h, wk, local.at[3]),
        pltpu.make_async_copy(wv_h, wv, local.at[4]),
        pltpu.make_async_copy(
            cache, kcc.at[:, pl.ds(pl.multiple_of(c * CAP, 64), CAP), :], local.at[5]
        ),
    ] + [
        pltpu.make_async_copy(wo_h.at[:, i * W : (i + 1) * W], wo.at[i], local.at[6 + i])
        for i in range(TP)
    ]
    for load in loads:
        load.start()

    barrier = pltpu.get_barrier_semaphore()
    for p in peers:
        pl.semaphore_signal(
            barrier, inc=1, device_id={"seq": s_idx, "tp": p}, device_id_type=pl.DeviceIdType.MESH
        )
    pl.semaphore_signal(
        barrier, inc=1, device_id={"seq": partner, "tp": t}, device_id_type=pl.DeviceIdType.MESH
    )

    def greet(i, carry):
        other = ((chip + i) % CHIPS) * CN + c
        pl.semaphore_signal(
            barrier, inc=1, device_id={"seq": other, "tp": t}, device_id_type=pl.DeviceIdType.MESH
        )
        return carry

    lax.fori_loop(1, CHIPS, greet, 0)

    r = iota((ALL, 128), 0)
    low_p = s_idx * BLK + r
    high_p = (2 * CHIPS * CN - 1 - s_idx) * BLK + r - BLK
    low_c = CACHED + s_idx * CBLK + r - ROWS
    high_c = CACHED + (2 * CHIPS * CN - 1 - s_idx) * CBLK + r - ROWS - CBLK
    pos = jnp.where(
        r < BLK, low_p, jnp.where(r < ROWS, high_p, jnp.where(r < ROWS + CBLK, low_c, high_c))
    )
    angle = pos.astype(F32) * inv[...]
    cos[...] = jnp.cos(angle)
    sine = jnp.sin(angle)
    sin[...] = jnp.where(iota((ALL, 128), 1) < HD // 2, -sine, sine)
    pad0 = 2 * CAP + 2 * CROWS
    kcc[:, pad0:, :] = jnp.zeros((2, CKEYS - pad0, W), BF16)

    pl.semaphore_wait(barrier, len(peers) + 1 + CHIPS - 1)

    sends = []
    for i in (6, 5, 4, 3, 2, 1, 0):
        a = remote(prompt, xg.at[t], tp_ss.at[i], tp_rs.at[t], tp=peers[i])
        b = remote(cont, xc.at[t], tpc_ss.at[i], tpc_rs.at[t], tp=peers[i])
        a.start()
        b.start()
        sends += [a, b]
    cache_send = remote(
        cache, kcc.at[:, pl.ds(pl.multiple_of(c * CAP, 64), CAP), :],
        core_ss.at[0], core_rs.at[0], seq=partner,
    )
    cache_send.start()

    for load in loads[:5]:
        load.wait()
    qp = jnp.zeros((ALL, W), F32)
    kp = jnp.zeros((ALL, W), F32)
    vp = jnp.zeros((ALL, W), F32)
    for i in range(-1, 7):
        if i >= 0:
            src = peers[i]
            remote(prompt, xg.at[src], tp_ss.at[i], tp_rs.at[src], tp=src).wait_recv()
            remote(cont, xc.at[src], tpc_ss.at[i], tpc_rs.at[src], tp=src).wait_recv()
        else:
            src = t
        rows = jnp.concatenate(
            [
                xg[src].reshape(ROWS, W),
                xc[src].astype(F32).reshape(CROWS, W).astype(BF16),
            ],
            0,
        )
        ks = pl.ds(pl.multiple_of(src * W, W), W)
        qp += jnp.dot(rows, wq[ks, :], preferred_element_type=F32)
        kp += jnp.dot(rows, wk[ks, :], preferred_element_type=F32)
        vp += jnp.dot(rows, wv[ks, :], preferred_element_type=F32)

    lane = iota((ALL, 128), 1)

    def total_squares(columns, phase):
        stat = jnp.zeros((ALL, 128), F32)
        for j, col in enumerate(columns):
            stat = jnp.where(lane == j, col, stat)
        stat = jnp.concatenate([stat, jnp.zeros((256 - ALL, 128), F32)], 0)
        mine = stat.T[:8, :]
        sq_out[phase] = mine
        out = []
        for i in range(7):
            d = remote(
                sq_out.at[phase], sq_in.at[phase, t], sq_ss.at[phase, i], sq_rs.at[phase, t],
                tp=peers[i],
            )
            d.start()
            out.append(d)
        total = mine
        for i in range(7):
            remote(
                sq_out.at[phase], sq_in.at[phase, peers[i]], sq_ss.at[phase, i],
                sq_rs.at[phase, peers[i]], tp=peers[i],
            ).wait_recv()
            total = total + sq_in[phase, peers[i]]
        back = jnp.concatenate([total, jnp.zeros((120, 256), F32)], 0).T
        return [back[:ALL, j : j + 1] for j in range(len(columns))], out

    (q_sq, k_sq), more = total_squares(
        [jnp.sum(qp * qp, -1, keepdims=True), jnp.sum(kp * kp, -1, keepdims=True)], 0
    )
    sends += more
    qn = qp * lax.rsqrt(q_sq / D + EPS) * qgain[...]
    kn = kp * lax.rsqrt(k_sq / D + EPS) * kgain[...]

    def rotate(field, scale):
        outs = []
        for h in range(2):
            f = field[:, h * HD : (h + 1) * HD]
            g = f * cos[...] + pltpu.roll(f, HD // 2, 1) * sin[...]
            outs.append((g * scale if scale is not None else g).astype(BF16))
        return jnp.concatenate(outs, -1)

    queries = rotate(qn, QSCALE)
    keys = rotate(kn, None)
    values = vp.astype(BF16)
    here = YN * 0 + 2 * y + c
    own = pl.ds(pl.multiple_of(here * BLK, BLK), BLK)
    qcg[chip] = queries[ROWS:]
    qg[z] = queries[:ROWS]
    for kv, field in ((0, keys), (1, values)):
        kvg[kv, 0, own, :] = field[:BLK]
        kvg[kv, 1, own, :] = field[BLK:ROWS]
        kcc[kv, pl.ds(pl.multiple_of(2 * CAP + c * CROWS, CROWS), CROWS), :] = field[ROWS:]

    def cont_q(i, other):
        return remote(qcg.at[chip], qcg.at[chip], qc_ss.at[i], qc_rs.at[chip],
                      seq=other * CN + c)

    def start_cont_q(i, carry):
        cont_q(i, (chip + i) % CHIPS).start()
        return carry

    lax.fori_loop(1, CHIPS, start_cont_q, 0)
    new_rows = kcc.at[:, pl.ds(pl.multiple_of(2 * CAP + c * CROWS, CROWS), CROWS), :]
    new_send = remote(new_rows, new_rows, core_ss.at[1], core_rs.at[1], seq=partner)
    new_send.start()
    sends += [cache_send, new_send]

    for i in (2, 1, 3):
        d = remote(qg.at[z], qg.at[z], q_ss.at[i], q_rs.at[z], seq=seq_of((z + i) % ZN, y, c))
        d.start()
        sends.append(d)

    def piece(origin_y, core, kv):
        rows = pl.ds(pl.multiple_of((2 * origin_y + core) * BLK, BLK), BLK)
        return kvg.at[kv, :, rows, :]

    right, left = seq_of(z, (y + 1) % YN, c), seq_of(z, (y + YN - 1) % YN, c)

    def ring(direction, step, kv, origin):
        return remote(
            piece(origin, c, kv), piece(origin, c, kv), ring_ss.at[direction, step, kv],
            ring_rs.at[direction, step, kv], seq=right if direction == 0 else left,
        )

    def pair(origin, core, kv):
        return remote(
            piece(origin, core, kv), piece(origin, core, kv),
            pair_ss.at[origin, kv], pair_rs.at[origin, kv], seq=partner,
        )

    def launch(step):
        for kv in range(2):
            for direction in range(2):
                if step == 4 and kv != direction:
                    continue
                origin = (y + (YN - step + 1 if direction == 0 else step - 1)) % YN
                if step > 1:
                    ring(direction, step - 1, kv, origin).wait_recv()
                d = ring(direction, step, kv, origin)
                d.start()
                sends.append(d)
                if step > 1 or direction == 0:
                    e = pair(origin, c, kv)
                    e.start()
                    sends.append(e)
            if step == 4:
                other = 1 - kv
                origin = (y + (YN - 3 if other == 0 else 3)) % YN
                ring(other, 3, kv, origin).wait_recv()
                e = pair(origin, c, kv)
                e.start()
                sends.append(e)

    launch(1)
    launch(2)
    launch(3)

    loads[5].wait()
    remote(
        cache, kcc.at[:, pl.ds(pl.multiple_of((1 - c) * CAP, 64), CAP), :],
        core_ss.at[0], core_rs.at[0], seq=partner,
    ).wait_recv()
    other_rows = kcc.at[:, pl.ds(pl.multiple_of(2 * CAP + (1 - c) * CROWS, CROWS), CROWS), :]
    remote(other_rows, other_rows, core_ss.at[1], core_rs.at[1], seq=partner).wait_recv()

    def wait_cont_q(i, carry):
        other = (chip + i) % CHIPS
        remote(qcg.at[other], qcg.at[other], qc_ss.at[i], qc_rs.at[other],
               seq=other * CN + c).wait_recv()
        return carry

    lax.fori_loop(1, CHIPS, wait_cont_q, 0)
    n = iota((1, CKEYS), 1)
    dead = 1 << 30
    j = n - 2 * CAP
    key_dev = chip * CN + j // CROWS
    in_block = j % CROWS
    new_pos = jnp.where(
        in_block < CBLK,
        key_dev * CBLK + in_block,
        (2 * CHIPS * CN - 1 - key_dev) * CBLK + in_block - CBLK,
    )
    key_pos = jnp.where(
        n < CAP,
        jnp.where(n < lengths[chip * CN], -1, dead),
        jnp.where(
            n < 2 * CAP,
            jnp.where(n - CAP < lengths[chip * CN + 1], -1, dead),
            jnp.where(n < pad0, new_pos, dead),
        ),
    )

    def cont_block(b, carry):
        rq = b * 128 + iota((128, 1), 0)
        dev = (rq // CROWS) * CN + c
        off = rq % CROWS
        q_pos = jnp.where(
            off < CBLK, dev * CBLK + off, (2 * CHIPS * CN - 1 - dev) * CBLK + off - CBLK
        )
        allowed = key_pos <= q_pos
        q = qcg[pl.ds(b * 8, 8)].reshape(128, W)
        parts = [
            attend(
                q[:, h * HD : (h + 1) * HD],
                kcc[0, :, h * HD : (h + 1) * HD],
                kcc[1, :, h * HD : (h + 1) * HD],
                allowed,
            )
            for h in range(2)
        ]
        oc_out[pl.ds(b * 8, 8)] = message(parts).reshape(8, CROWS, MSG)
        return carry

    lax.fori_loop(0, 4, cont_block, 0)

    launch(4)

    def cont_o(i, other):
        return remote(oc_out.at[other], oc_in.at[chip], oc_ss.at[i], oc_rs.at[chip],
                      seq=other * CN + c)

    def start_cont_o(i, carry):
        cont_o(i, (chip + i) % CHIPS).start()
        return carry

    lax.fori_loop(1, CHIPS, start_cont_o, 0)

    far = (y + 4) % YN
    for kv in range(2):
        ring(kv, 4, kv, far).wait_recv()
        e = pair(far, c, kv)
        e.start()
        sends.append(e)
    for i in (2, 1, 3):
        src = (z + i) % ZN
        remote(qg.at[src], qg.at[src], q_ss.at[i], q_rs.at[src],
               seq=seq_of(src, y, c)).wait_recv()
    for origin in range(YN):
        for kv in range(2):
            remote(
                piece(origin, 1 - c, kv), piece(origin, 1 - c, kv),
                pair_ss.at[origin, kv], pair_rs.at[origin, kv], seq=partner,
            ).wait_recv()

    n2 = iota((1, 2 * KEYS), 1)
    hi_n = n2 - KEYS
    top = 2 * CHIPS * CN - 1
    key_pos2 = jnp.where(
        n2 < KEYS,
        z * KEYS + n2,
        (top - z * (YN * CN) - hi_n // BLK) * BLK + hi_n % BLK,
    )

    def prompt_block(i, carry):
        zq = (z + i) % ZN
        dev = zq * (YN * CN) + here
        rq = iota((ROWS, 1), 0)
        q_pos = jnp.where(rq < BLK, dev * BLK + rq, (top - dev) * BLK + rq - BLK)
        allowed = key_pos2 <= q_pos
        q = qg[zq]
        parts = [
            attend(
                q[:, h * HD : (h + 1) * HD],
                kvg[0, :, :, h * HD : (h + 1) * HD].reshape(2 * KEYS, HD),
                kvg[1, :, :, h * HD : (h + 1) * HD].reshape(2 * KEYS, HD),
                allowed,
            )
            for h in range(2)
        ]
        op_out[zq] = message(parts)
        return carry

    def prompt_o(i):
        return remote(op_out.at[(z + i) % ZN], op_in.at[z], op_ss.at[i], op_rs.at[z],
                      seq=seq_of((z + i) % ZN, y, c))

    for i in (2, 1, 3):
        prompt_block(i, 0)
        d = prompt_o(i)
        d.start()
        sends.append(d)
    prompt_block(0, 0)

    ro = iota((128, 2 * KEYS), 0)
    co = iota((128, 2 * KEYS), 1)
    jj = ro % 16
    want = (ro // 32) * 16 + here
    pick_row = jnp.where(ro % 32 < 16, jj * BLK, KEYS + (15 - jj) * BLK) + want
    onehot = jnp.where(co == pick_row, 1.0, 0.0).astype(BF16)
    for kv in range(2):
        rows = jnp.dot(onehot, kvg[kv].reshape(2 * KEYS, W), preferred_element_type=F32)
        kv_s[:, kv] = rows.astype(BF16).reshape(ZN, 2, 16, W)
    for i in (2, 1, 3):
        dst = (z + i) % ZN
        d = remote(kv_s.at[dst], kv_r.at[z], kv_ss.at[i], kv_rs.at[z], seq=seq_of(dst, y, c))
        d.start()
        sends.append(d)

    def wait_cont_o(i, carry):
        other = (chip + i) % CHIPS
        remote(oc_out.at[other], oc_in.at[other], oc_ss.at[i], oc_rs.at[other],
               seq=other * CN + c).wait_recv()
        return carry

    lax.fori_loop(1, CHIPS, wait_cont_o, 0)
    oc_in[chip] = oc_out[chip]
    att[ROWS:, :] = combine([oc_in[i] for i in range(CHIPS)])
    for i in (1, 3, 2):
        src = (z + i) % ZN
        remote(op_out.at[src], op_in.at[src], op_ss.at[i], op_rs.at[src],
               seq=seq_of(src, y, c)).wait_recv()
    att[:ROWS, :] = combine([op_out[z]] + [op_in[(z + i) % ZN] for i in (1, 3, 2)])

    for load in loads[6:]:
        load.wait()
    a = att[...]
    for i in (6, 5, 4, 3, 2, 1, 0):
        p = peers[i]
        pr_out[p] = jnp.dot(a, wo[p], preferred_element_type=F32).astype(BF16)
        d = remote(pr_out.at[p], pr_in.at[t], pr_ss.at[i], pr_rs.at[t], tp=p)
        d.start()
        sends.append(d)
    proj = jnp.dot(a, wo[t], preferred_element_type=F32).astype(BF16).astype(F32)
    for i in range(7):
        p = peers[i]
        remote(pr_out.at[p], pr_in.at[p], pr_ss.at[i], pr_rs.at[p], tp=p).wait_recv()
        proj = proj + pr_in[p].astype(F32)

    (p_sq,), more = total_squares([jnp.sum(proj * proj, -1, keepdims=True)], 1)
    sends += more
    normed = proj * lax.rsqrt(p_sq / D + EPS) * pgain[...]
    hid_p[...] = (xg[t].astype(F32) + normed[:ROWS].reshape(2, BLK, W)).astype(BF16)
    hid_c[...] = (xc[t].astype(F32) + normed[ROWS:].reshape(2, CBLK, W)).astype(BF16)

    for i in (1, 3, 2):
        src = (z + i) % ZN
        remote(kv_s.at[src], kv_r.at[src], kv_ss.at[i], kv_rs.at[src],
               seq=seq_of(src, y, c)).wait_recv()
    kv_r[z] = kv_s[z]
    for src in range(ZN):
        for kv in range(2):
            kv_out[kv, 16 * src : 16 * src + 16, :] = kv_r[src, kv, 0]
            kv_out[kv, 112 - 16 * src : 128 - 16 * src, :] = kv_r[src, kv, 1]

    for d in sends:
        d.wait_send()

    def drain(i, carry):
        cont_q(i, (chip + i) % CHIPS).wait_send()
        cont_o(i, (chip + i) % CHIPS).wait_send()
        return carry

    lax.fori_loop(1, CHIPS, drain, 0)


def per_device(
    prompt_states, cont_states, cache_kv, cache_lengths, w_query, w_key, w_value, w_out,
    q_gain, k_gain, post_gain,
):
    half = HD // 2
    freq = THETA ** (-(np.arange(half) * 2.0 / HD))
    inv = jnp.asarray(np.concatenate([freq, freq])[None, :].astype(np.float32))
    any_ = pl.BlockSpec(memory_space=pl.ANY)
    vmem = pl.BlockSpec(memory_space=pltpu.VMEM)
    smem = pl.BlockSpec(memory_space=pltpu.SMEM)
    dma = pltpu.SemaphoreType.DMA
    hid_p, hid_c, kv = pl.pallas_call(
        kernel,
        out_shape=(
            jax.ShapeDtypeStruct((2, BLK, W), BF16),
            jax.ShapeDtypeStruct((2, CBLK, W), BF16),
            jax.ShapeDtypeStruct((2, 2 * BLK, W), BF16),
        ),
        in_specs=[any_, any_, any_, smem, any_, any_, any_, any_, vmem, vmem, vmem, vmem],
        out_specs=(vmem, vmem, vmem),
        scratch_shapes=[
            pltpu.VMEM((D, W), BF16),
            pltpu.VMEM((D, W), BF16),
            pltpu.VMEM((D, W), BF16),
            pltpu.VMEM((TP, W, W), BF16),
            pltpu.VMEM((TP, 2, BLK, W), BF16),
            pltpu.VMEM((TP, 2, CBLK, W), BF16),
            pltpu.VMEM((ALL, 128), F32),
            pltpu.VMEM((ALL, 128), F32),
            pltpu.VMEM((2, 8, 256), F32),
            pltpu.VMEM((2, TP, 8, 256), F32),
            pltpu.VMEM((ZN, ROWS, W), BF16),
            pltpu.VMEM((2, 2, KEYS, W), BF16),
            pltpu.VMEM((CHIPS, CROWS, W), BF16),
            pltpu.VMEM((2, CKEYS, W), BF16),
            pltpu.VMEM((CHIPS, CROWS, MSG), BF16),
            pltpu.VMEM((CHIPS, CROWS, MSG), BF16),
            pltpu.VMEM((ZN, ROWS, MSG), BF16),
            pltpu.VMEM((ZN, ROWS, MSG), BF16),
            pltpu.VMEM((ZN, 2, 2, 16, W), BF16),
            pltpu.VMEM((ZN, 2, 2, 16, W), BF16),
            pltpu.VMEM((ALL, W), BF16),
            pltpu.VMEM((TP, ALL, W), BF16),
            pltpu.VMEM((TP, ALL, W), BF16),
            dma((6 + TP,)),
            dma((7,)), dma((TP,)), dma((7,)), dma((TP,)),
            dma((2, 7)), dma((2, TP)),
            dma((2,)), dma((2,)),
            dma((CHIPS,)), dma((CHIPS,)),
            dma((ZN,)), dma((ZN,)),
            dma((2, 5, 2)), dma((2, 5, 2)),
            dma((YN, 2)), dma((YN, 2)),
            dma((CHIPS,)), dma((CHIPS,)),
            dma((ZN,)), dma((ZN,)),
            dma((ZN,)), dma((ZN,)),
            dma((7,)), dma((TP,)),
        ],
        compiler_params=pltpu.CompilerParams(
            collective_id=0, has_side_effects=True, vmem_limit_bytes=60 * 1024 * 1024
        ),
        name="block",
    )(
        prompt_states[:, 0], cont_states[:, 0], cache_kv[:, 0], cache_lengths,
        w_query, w_key, w_value, w_out,
        q_gain[None], k_gain[None], post_gain[None], inv,
    )
    return hid_p[:, None], hid_c[:, None], kv[:, None]


def solution(mesh):
    return jax.shard_map(
        per_device,
        mesh=mesh,
        in_specs=(
            P(None, "seq", None, "tp"),
            P(None, "seq", None, "tp"),
            P(None, "seq", None, "tp"),
            P(),
            P(None, "tp"),
            P(None, "tp"),
            P(None, "tp"),
            P("tp", None),
            P("tp"),
            P("tp"),
            P("tp"),
        ),
        out_specs=(
            P(None, "seq", None, "tp"),
            P(None, "seq", None, "tp"),
            P(None, "seq", None, "tp"),
        ),
        check_vma=False,
    )
```

```python
import math
import jax
import jax.numpy as jnp
import numpy as np
from jax import lax
from jax.experimental import pallas as pl
from jax.experimental.pallas import tpu as pltpu
from jax.sharding import PartitionSpec as P

HD = 128
EPS = 1e-06
THETA = 500000.0
NEG = -1e30
ZN, YN, CN, TP = 4, 8, 2, 8
BLK, CBLK, CAP = 64, 8, 448
ROWS = 2 * BLK
CROWS = 2 * CBLK
ALL = ROWS + CROWS
W = 256
D = 2048
CACHED = 14336
KEYS = YN * CN * BLK
QUAD = 4
CGROUP = ZN * YN // 2
CKEYS = 1920
MSG = W + 128
QSCALE = math.log2(math.e) / math.sqrt(HD)
F32, BF16 = jnp.float32, jnp.bfloat16


def iota(shape, dim):
    return lax.broadcasted_iota(jnp.int32, shape, dim)


def attend(q, k, v, allowed, k_scale=None):
    s = lax.dot_general(q, k, (((1,), (1,)), ((), ())), preferred_element_type=F32)
    if k_scale is not None:
        s = s * k_scale
    s = jnp.where(allowed, s, NEG)
    m = jnp.max(s, -1, keepdims=True).astype(BF16).astype(F32)
    p = jnp.exp2(s - jnp.maximum(m, -1e29))
    total = jnp.sum(p, -1, keepdims=True)
    out = jnp.dot(p.astype(BF16), v, preferred_element_type=F32)
    return out, m, total


def message(parts):
    rows = parts[0][0].shape[0]
    lane = iota((rows, 128), 1)
    stats = jnp.zeros((rows, 128), F32)
    for h, (_, m, total) in enumerate(parts):
        high = total.astype(BF16).astype(F32)
        stats = jnp.where(lane == 3 * h, m, stats)
        stats = jnp.where(lane == 3 * h + 1, high, stats)
        stats = jnp.where(lane == 3 * h + 2, total - high, stats)
    return jnp.concatenate([p[0].astype(BF16) for p in parts] + [stats.astype(BF16)], -1)


def combine(pieces, stats):
    outs = []
    for h in range(2):
        top = stats[0][h][0]
        for st in stats[1:]:
            top = jnp.maximum(top, st[h][0])
        num, den = 0.0, 0.0
        for p, st in zip(pieces, stats):
            w = jnp.exp2(st[h][0] - top)
            num = num + w * p[:, h * HD : (h + 1) * HD].astype(F32)
            den = den + w * st[h][1]
        outs.append(num / den)
    return jnp.concatenate(outs, -1).astype(BF16)


def message_stats(piece):
    st = piece[:, W:].astype(F32)
    return [
        (st[:, 3 * h : 3 * h + 1], st[:, 3 * h + 1 : 3 * h + 2] + st[:, 3 * h + 2 : 3 * h + 3])
        for h in range(2)
    ]


def kernel(
    prompt, cont, cache, lengths, wq_h, wk_h, wv_h, wo_h, qgain, kgain, pgain, inv,
    hid_p, hid_c, kv_out,
    wq, wk, wv, wo, xg, xc, cos, sin, sq_out, sq_in, qg, kvg, qcg, kcc,
    oc_out, oc_in, op_out, op_in, os_out, os_in, kv_s, kv_r, att, pr_out, pr_in,
    ks_out, ks_in,
    local, tp_ss, tp_rs, tpc_ss, tpc_rs, sq_ss, sq_rs, cache_ss, cache_rs, new_ss, new_rs, ready,
    qc_ss, qc_rs, q_ss, q_rs, ring_ss, ring_rs, pair_ss, pair_rs,
    oc_ss, oc_rs, op_ss, op_rs, os_ss, os_rs, kv_ss, kv_rs, pr_ss, pr_rs,
    ks_ss, ks_rs,
):
    s_idx = lax.axis_index("seq")
    t = lax.axis_index("tp")
    z = s_idx // (YN * CN)
    y = (s_idx // CN) % YN
    c = s_idx % CN
    x, zl = t // 2, t % 2

    def seq_of(z_, y_, c_):
        return (z_ * YN + y_) * CN + c_

    def remote(src, dst, ss, rs, seq=None, tp=None):
        dev = {"seq": s_idx if seq is None else seq, "tp": t if tp is None else tp}
        return pltpu.make_async_remote_copy(
            src_ref=src, dst_ref=dst, send_sem=ss, recv_sem=rs,
            device_id=dev, device_id_type=pl.DeviceIdType.MESH,
        )

    partner = s_idx + 1 - 2 * c
    b = y % 2
    slot = 2 * b + c
    base = s_idx - slot
    twin = seq_of(z, y + 1 - 2 * b, c)
    cross = seq_of(z, y + 1 - 2 * b, 1 - c)
    twin_slot = 2 * (1 - b) + c
    group = z * (YN // 2) + y // 2

    def member(i):
        return seq_of(i // (YN // 2), (i % (YN // 2)) * 2 + b, c)

    def cache_rows(j):
        return kcc.at[:, pl.ds(pl.multiple_of(j * CAP, 64), CAP), :]

    def new_rows(j):
        return kcc.at[:, pl.ds(pl.multiple_of(QUAD * CAP + j * CROWS, CROWS), CROWS), :]

    hops = [(0, 1), (1, 0), (3, 0), (1, 1), (3, 1), (2, 0), (2, 1)]
    peers = [((x + dx) % 4) * 2 + (zl + dz) % 2 for dx, dz in hops]

    loads = [
        pltpu.make_async_copy(prompt, xg.at[t], local.at[0]),
        pltpu.make_async_copy(cont, xc.at[t], local.at[1]),
        pltpu.make_async_copy(wq_h, wq, local.at[2]),
        pltpu.make_async_copy(wk_h, wk, local.at[3]),
        pltpu.make_async_copy(wv_h, wv, local.at[4]),
        pltpu.make_async_copy(cache, cache_rows(slot), local.at[5]),
    ] + [
        pltpu.make_async_copy(wo_h.at[:, i * W : (i + 1) * W], wo.at[i], local.at[6 + i])
        for i in range(TP)
    ]
    for load in loads:
        load.start()

    def signal(sem, seq, tp):
        pl.semaphore_signal(
            sem, inc=1, device_id={"seq": seq, "tp": tp}, device_id_type=pl.DeviceIdType.MESH
        )

    barrier = pltpu.get_barrier_semaphore()
    here = 2 * y + c
    greeted = [(s_idx, p) for p in peers]
    greeted += [(z * (YN * CN) + (here + i) % (YN * CN), t) for i in range(1, YN * CN)]
    greeted += [(seq_of((z + i) % ZN, y, c), t) for i in (1, 2, 3)]
    for seq, tp in greeted:
        signal(barrier, seq, tp)

    pl.semaphore_wait(barrier, len(greeted))
    for i in (1, 2, 3):
        signal(ready, seq_of((z + i) % ZN, y, c), t)

    sends = []
    def go(*copies):
        for d in copies:
            d.start()
            sends.append(d)

    def rows_to(i):
        return remote(prompt, xg.at[t], tp_ss.at[i], tp_rs.at[t], tp=peers[i])

    def new_to(i):
        return remote(cont, xc.at[t], tpc_ss.at[i], tpc_rs.at[t], tp=peers[i])

    for i in (6, 5, 4, 3, 2, 1, 0):
        go(rows_to(i), new_to(i))
    for i, seq in ((0, twin), (1, partner)):
        d = remote(cache, cache_rows(slot), cache_ss.at[i], cache_rs.at[slot], seq=seq)
        d.start()
        sends.append(d)

    r = iota((ALL, 128), 0)
    low_p = s_idx * BLK + r
    high_p = (2 * CN * YN * ZN - 1 - s_idx) * BLK + r - BLK
    low_c = CACHED + s_idx * CBLK + r - ROWS
    high_c = CACHED + (2 * CN * YN * ZN - 1 - s_idx) * CBLK + r - ROWS - CBLK
    pos = jnp.where(
        r < BLK, low_p, jnp.where(r < ROWS, high_p, jnp.where(r < ROWS + CBLK, low_c, high_c))
    )
    angle = pos.astype(F32) * inv[...]
    cos[...] = jnp.cos(angle)
    sine = jnp.sin(angle)
    sin[...] = jnp.where(iota((ALL, 128), 1) < HD // 2, -sine, sine)
    pad0 = QUAD * (CAP + CROWS)
    kcc[:, pad0:, :] = jnp.zeros((2, CKEYS - pad0, W), BF16)

    for load in loads[:5]:
        load.wait()
    qp = jnp.zeros((ALL, W), F32)
    kp = jnp.zeros((ALL, W), F32)
    vp = jnp.zeros((ALL, W), F32)
    for i in range(-1, 7):
        if i < 0:
            src = t
        else:
            src = peers[i]
            remote(prompt, xg.at[src], tp_ss.at[i], tp_rs.at[src], tp=src).wait_recv()
            remote(cont, xc.at[src], tpc_ss.at[i], tpc_rs.at[src], tp=src).wait_recv()
        rows = jnp.concatenate(
            [
                xg[src].reshape(ROWS, W),
                xc[src].astype(F32).reshape(CROWS, W).astype(BF16),
            ],
            0,
        )
        ks = pl.ds(pl.multiple_of(src * W, W), W)
        qp += jnp.dot(rows, wq[ks, :], preferred_element_type=F32)
        kp += jnp.dot(rows, wk[ks, :], preferred_element_type=F32)
        vp += jnp.dot(rows, wv[ks, :], preferred_element_type=F32)

    lane = iota((ALL, 128), 1)

    def send_squares(columns, phase):
        stat = jnp.zeros((ALL, 128), F32)
        for j, col in enumerate(columns):
            stat = jnp.where(lane == j, col, stat)
        stat = jnp.concatenate([stat, jnp.zeros((256 - ALL, 128), F32)], 0)
        sq_out[phase] = stat.T[:8, :]
        for i in (6, 5, 4, 3, 2, 1, 0):
            d = remote(
                sq_out.at[phase], sq_in.at[phase, t], sq_ss.at[phase, i], sq_rs.at[phase, t],
                tp=peers[i],
            )
            d.start()
            sends.append(d)

    def total_squares(count, phase):
        total = sq_out[phase]
        for i in range(7):
            remote(
                sq_out.at[phase], sq_in.at[phase, peers[i]], sq_ss.at[phase, i],
                sq_rs.at[phase, peers[i]], tp=peers[i],
            ).wait_recv()
            total = total + sq_in[phase, peers[i]]
        back = jnp.concatenate([total, jnp.zeros((120, 256), F32)], 0).T
        return [back[:ALL, j : j + 1] for j in range(count)]

    send_squares([jnp.sum(qp * qp, -1, keepdims=True), jnp.sum(kp * kp, -1, keepdims=True)], 0)

    own = pl.ds(pl.multiple_of(here * BLK, BLK), BLK)

    def rotate(field):
        outs = []
        for h in range(2):
            f = field[:, h * HD : (h + 1) * HD]
            outs.append(f * cos[...] + pltpu.roll(f, HD // 2, 1) * sin[...])
        return jnp.concatenate(outs, -1)

    def keep(kv, field):
        kvg[kv, 0, own, :] = field[:BLK]
        kvg[kv, 1, own, :] = field[BLK:ROWS]

    def piece(origin_y, core, kv, half):
        rows = pl.ds(pl.multiple_of((2 * origin_y + core) * BLK, BLK), BLK)
        return kvg.at[kv, half, rows, :]

    def along(hop, direction, dist, kv, half, origin):
        step = dist if direction == 0 else YN - dist
        return remote(
            piece(origin, c, kv, half), piece(origin, c, kv, half),
            ring_ss.at[direction, hop, kv, half], ring_rs.at[direction, hop, kv, half],
            seq=seq_of(z, (y + step) % YN, c),
        )

    def pair(origin, core, kv, half):
        return remote(
            piece(origin, core, kv, half), piece(origin, core, kv, half),
            pair_ss.at[origin, kv, half], pair_rs.at[origin, kv, half], seq=partner,
        )

    def start_pair(origin, kv, half):
        d = pair(origin, c, kv, half)
        d.start()
        sends.append(d)

    def launch(kv):
        for dist in (2, 1):
            for half in range(2):
                for direction in range(2):
                    go(along(dist, direction, dist, kv, half, y))
        for half in range(2):
            start_pair(y, kv, half)

    def came_from(direction, dist):
        return (y + (YN - dist if direction == 0 else dist)) % YN

    def forward(kv):
        for half in range(2):
            for direction in range(2):
                origin = came_from(direction, 2)
                along(2, direction, 2, kv, half, origin).wait_recv()
                if direction == half:
                    go(along(4, direction, 2, kv, half, origin))
                go(along(3, direction, 1, kv, half, origin))
                start_pair(origin, kv, half)
        for half in range(2):
            for direction in range(2):
                origin = came_from(direction, 1)
                along(1, direction, 1, kv, half, origin).wait_recv()
                start_pair(origin, kv, half)

    def finish(kv):
        for half in range(2):
            for direction in range(2):
                origin = came_from(direction, 3)
                along(3, direction, 1, kv, half, origin).wait_recv()
                start_pair(origin, kv, half)
            origin = came_from(half, 4)
            along(4, half, 2, kv, half, origin).wait_recv()
            start_pair(origin, kv, half)

    def wait_pairs(kv):
        for origin in range(YN):
            for half in range(2):
                pair(origin, 1 - c, kv, half).wait_recv()

    values = vp.astype(BF16)
    keep(1, values)
    launch(1)
    turned = rotate(kp * kgain[...])
    keep(0, turned.astype(BF16))
    launch(0)
    q_sq, k_sq = total_squares(2, 0)
    q_scale = lax.rsqrt(q_sq / D + EPS)
    k_scale = lax.rsqrt(k_sq / D + EPS)
    ks_out[...] = jnp.where(lane[:ROWS] == 0, k_scale[:ROWS], 0.0).T[:8, :]
    new_rows(slot)[0] = (turned[ROWS:] * k_scale[ROWS:]).astype(BF16)
    new_rows(slot)[1] = values[ROWS:]
    queries = (rotate(qp * q_scale * qgain[...]) * QSCALE).astype(BF16)

    def send_scale(i, other):
        return remote(ks_out, ks_in.at[here], ks_ss.at[i], ks_rs.at[here],
                      seq=z * (YN * CN) + other)

    def start_scale(i, carry):
        send_scale(i, (here + i) % (YN * CN)).start()
        return carry

    lax.fori_loop(1, YN * CN, start_scale, 0)
    ks_in[here] = ks_out[...]
    forward(1)
    qcg[group] = queries[ROWS:]
    qg[z] = queries[:ROWS].reshape(2, BLK, W)

    pl.semaphore_wait(ready, 3)

    def cont_q(i, other):
        return remote(qcg.at[group], qcg.at[group], qc_ss.at[i], qc_rs.at[group],
                      seq=member(other))

    def start_cont_q(i, carry):
        cont_q(i, (group + i) % CGROUP).start()
        return carry

    lax.fori_loop(1, CGROUP, start_cont_q, 0)
    for i, seq in ((0, partner), (1, twin), (2, cross)):
        d = remote(new_rows(slot), new_rows(slot), new_ss.at[i], new_rs.at[slot], seq=seq)
        d.start()
        sends.append(d)

    for i in (2, 1, 3):
        go(remote(qg.at[z], qg.at[z], q_ss.at[i], q_rs.at[z], seq=seq_of((z + i) % ZN, y, c)))

    forward(0)
    remote(cache, cache_rows(twin_slot), cache_ss.at[0], cache_rs.at[twin_slot],
           seq=twin).wait_recv()
    d = remote(cache_rows(twin_slot), cache_rows(twin_slot), cache_ss.at[2],
               cache_rs.at[twin_slot], seq=partner)
    d.start()
    sends.append(d)
    loads[5].wait()
    for i, j in ((1, 2 * b + 1 - c), (2, 2 * (1 - b) + 1 - c)):
        remote(cache, cache_rows(j), cache_ss.at[i], cache_rs.at[j], seq=partner).wait_recv()
    for i, j in ((0, 2 * b + 1 - c), (1, twin_slot), (2, 2 * (1 - b) + 1 - c)):
        remote(new_rows(j), new_rows(j), new_ss.at[i], new_rs.at[j], seq=partner).wait_recv()

    def wait_cont_q(i, carry):
        other = (group + i) % CGROUP
        remote(qcg.at[other], qcg.at[other], qc_ss.at[i], qc_rs.at[other],
               seq=member(other)).wait_recv()
        return carry

    lax.fori_loop(1, CGROUP, wait_cont_q, 0)
    top = 2 * CN * YN * ZN - 1
    n = iota((1, CKEYS), 1)
    dead = 1 << 30
    j = n - QUAD * CAP
    key_dev = base + j // CROWS
    in_block = j % CROWS
    new_pos = jnp.where(
        in_block < CBLK,
        key_dev * CBLK + in_block,
        (top - key_dev) * CBLK + in_block - CBLK,
    )
    key_pos = jnp.where((n >= QUAD * CAP) & (n < pad0), new_pos, dead)
    for i in range(QUAD):
        live = (n >= i * CAP) & (n < i * CAP + lengths[base + i])
        key_pos = jnp.where(live, -1, key_pos)

    def cont_block(blk, carry):
        rq = blk * 128 + iota((128, 1), 0)
        who = rq // CROWS
        dev = seq_of(who // (YN // 2), (who % (YN // 2)) * 2 + b, c)
        off = rq % CROWS
        q_pos = jnp.where(off < CBLK, dev * CBLK + off, (top - dev) * CBLK + off - CBLK)
        allowed = key_pos <= q_pos
        q = qcg[pl.ds(blk * 8, 8)].reshape(128, W)
        parts = [
            attend(
                q[:, h * HD : (h + 1) * HD],
                kcc[0, :, h * HD : (h + 1) * HD],
                kcc[1, :, h * HD : (h + 1) * HD],
                allowed,
            )
            for h in range(2)
        ]
        oc_out[pl.ds(blk * 8, 8)] = message(parts).reshape(8, CROWS, MSG)
        return carry

    cont_block(0, 0)
    finish(1)
    cont_block(1, 0)

    def cont_o(i, other):
        return remote(oc_out.at[other], oc_in.at[group], oc_ss.at[i], oc_rs.at[group],
                      seq=member(other))

    def start_cont_o(i, carry):
        cont_o(i, (group + i) % CGROUP).start()
        return carry

    lax.fori_loop(1, CGROUP, start_cont_o, 0)

    ro = iota((128, 2 * KEYS), 0)
    co = iota((128, 2 * KEYS), 1)
    jj = ro % 16
    want = (ro // 32) * 16 + here
    pick_row = jnp.where(ro % 32 < 16, jj * BLK, KEYS + (15 - jj) * BLK) + want
    onehot = jnp.where(co == pick_row, 1.0, 0.0).astype(BF16)

    def cyclic_rows(kv):
        rows = jnp.dot(onehot, kvg[kv].reshape(2 * KEYS, W), preferred_element_type=F32)
        if kv == 0:
            rows = rows * jnp.sum(jnp.where(co == pick_row, key_scale, 0.0), -1, keepdims=True)
        kv_s[kv] = rows.astype(BF16).reshape(ZN, 2, 16, W)
        for i in (2, 1, 3):
            dst = (z + i) % ZN
            d = remote(kv_s.at[kv, dst], kv_r.at[kv, z], kv_ss.at[kv, i], kv_rs.at[kv, z],
                       seq=seq_of(dst, y, c))
            d.start()
            sends.append(d)

    finish(0)
    wait_pairs(1)
    cyclic_rows(1)
    for i in (2, 1, 3):
        src = (z + i) % ZN
        remote(qg.at[src], qg.at[src], q_ss.at[i], q_rs.at[src],
               seq=seq_of(src, y, c)).wait_recv()

    def wait_scale(i, carry):
        other = (here + i) % (YN * CN)
        remote(ks_out, ks_in.at[other], ks_ss.at[i], ks_rs.at[other],
               seq=z * (YN * CN) + other).wait_recv()
        return carry

    lax.fori_loop(1, YN * CN, wait_scale, 0)
    low_half = iota((8, 128), 1) < BLK
    lows, highs = [], []
    for i in range(YN):
        first, second = ks_in[2 * i], ks_in[2 * i + 1]
        lows.append(jnp.where(low_half, first, pltpu.roll(second, BLK, 1))[:1])
        highs.append(jnp.where(low_half, pltpu.roll(first, BLK, 1), second)[:1])
    key_scale = jnp.concatenate(lows + highs, 1)
    wait_pairs(0)

    n2 = iota((1, 2 * KEYS), 1)
    hi_n = n2 - KEYS
    key_pos2 = jnp.where(
        n2 < KEYS,
        z * KEYS + n2,
        (top - z * (YN * CN) - hi_n // BLK) * BLK + hi_n % BLK,
    )

    def prompt_block(i, carry):
        zq = (z + i) % ZN
        dev = zq * (YN * CN) + here
        rq = iota((ROWS, 1), 0)
        q_pos = jnp.where(rq < BLK, dev * BLK + rq, (top - dev) * BLK + rq - BLK)
        allowed = key_pos2 <= q_pos
        q = qg[zq].reshape(ROWS, W)
        parts = [
            attend(
                q[:, h * HD : (h + 1) * HD],
                kvg[0, :, :, h * HD : (h + 1) * HD].reshape(2 * KEYS, HD),
                kvg[1, :, :, h * HD : (h + 1) * HD].reshape(2 * KEYS, HD),
                allowed,
                key_scale,
            )
            for h in range(2)
        ]
        op_out[zq] = jnp.concatenate([p[0].astype(BF16) for p in parts], -1).reshape(2, BLK, W)
        stats = jnp.zeros((ROWS, 128), F32)
        for h in range(2):
            stats = jnp.where(lane[:ROWS] == 2 * h, parts[h][1], stats)
            stats = jnp.where(lane[:ROWS] == 2 * h + 1, parts[h][2], stats)
        os_out[zq] = stats.T[:8, :]
        return carry

    def stats_o(i, dst):
        return remote(os_out.at[dst], os_in.at[z], os_ss.at[i], os_rs.at[z],
                      seq=seq_of(dst, y, c))

    def near_o(i, dst):
        return remote(op_out.at[dst], op_in.at[z], op_ss.at[i], op_rs.at[z],
                      seq=seq_of(dst, y, c))

    for i in (2, 1, 3):
        prompt_block(i, 0)
        dst = (z + i) % ZN
        go(near_o(i, dst), stats_o(i, dst))
    prompt_block(0, 0)
    cyclic_rows(0)

    def wait_cont_o(i, carry):
        other = (group + i) % CGROUP
        remote(oc_out.at[other], oc_in.at[other], oc_ss.at[i], oc_rs.at[other],
               seq=member(other)).wait_recv()
        return carry

    lax.fori_loop(1, CGROUP, wait_cont_o, 0)
    oc_in[group] = oc_out[group]
    cont_parts = [oc_in[i] for i in range(CGROUP)]
    att[ROWS:, :] = combine(cont_parts, [message_stats(p) for p in cont_parts])
    pieces, stats = [op_out[z].reshape(ROWS, W)], [os_out[z]]
    for i in (1, 3, 2):
        src = (z + i) % ZN
        remote(op_out.at[src], op_in.at[src], op_ss.at[i], op_rs.at[src],
               seq=seq_of(src, y, c)).wait_recv()
        remote(os_out.at[src], os_in.at[src], os_ss.at[i], os_rs.at[src],
               seq=seq_of(src, y, c)).wait_recv()
        pieces.append(op_in[src].reshape(ROWS, W))
        stats.append(os_in[src])
    cols = jnp.concatenate(stats + [jnp.zeros((96, 128), F32)], 0).T
    att[:ROWS, :] = combine(
        pieces,
        [
            [
                (cols[:, 8 * i + 2 * h : 8 * i + 2 * h + 1],
                 cols[:, 8 * i + 2 * h + 1 : 8 * i + 2 * h + 2])
                for h in range(2)
            ]
            for i in range(ZN)
        ],
    )

    for load in loads[6:]:
        load.wait()
    a = att[...]

    def project(p):
        return jnp.dot(a, wo[p], preferred_element_type=F32).astype(BF16)

    for i in (6, 5, 4, 3, 2, 1, 0):
        p = peers[i]
        pr_out[p] = project(p)
        go(remote(pr_out.at[p], pr_in.at[t], pr_ss.at[i], pr_rs.at[t], tp=p))
    proj = project(t).astype(F32)
    for i in range(7):
        p = peers[i]
        remote(pr_out.at[p], pr_in.at[p], pr_ss.at[i], pr_rs.at[p], tp=p).wait_recv()
        proj = proj + pr_in[p].astype(F32)

    send_squares([jnp.sum(proj * proj, -1, keepdims=True)], 1)
    (p_sq,) = total_squares(1, 1)
    normed = proj * lax.rsqrt(p_sq / D + EPS) * pgain[...]
    hid_p[...] = (xg[t].astype(F32) + normed[:ROWS].reshape(2, BLK, W)).astype(BF16)
    hid_c[...] = (xc[t].astype(F32) + normed[ROWS:].reshape(2, CBLK, W)).astype(BF16)

    for kv in range(2):
        for i in (1, 3, 2):
            src = (z + i) % ZN
            remote(kv_s.at[kv, src], kv_r.at[kv, src], kv_ss.at[kv, i], kv_rs.at[kv, src],
                   seq=seq_of(src, y, c)).wait_recv()
        kv_r[kv, z] = kv_s[kv, z]
        for src in range(ZN):
            kv_out[kv, 16 * src : 16 * src + 16, :] = kv_r[kv, src, 0]
            kv_out[kv, 112 - 16 * src : 128 - 16 * src, :] = kv_r[kv, src, 1]

    for d in sends:
        d.wait_send()

    def drain(i, carry):
        cont_q(i, (group + i) % CGROUP).wait_send()
        cont_o(i, (group + i) % CGROUP).wait_send()
        send_scale(i, (here + i) % (YN * CN)).wait_send()
        return carry

    lax.fori_loop(1, CGROUP, drain, 0)


def per_device(
    prompt_states, cont_states, cache_kv, cache_lengths, w_query, w_key, w_value, w_out,
    q_gain, k_gain, post_gain,
):
    half = HD // 2
    freq = THETA ** (-(np.arange(half) * 2.0 / HD))
    inv = jnp.asarray(np.concatenate([freq, freq])[None, :].astype(np.float32))
    any_ = pl.BlockSpec(memory_space=pl.ANY)
    vmem = pl.BlockSpec(memory_space=pltpu.VMEM)
    smem = pl.BlockSpec(memory_space=pltpu.SMEM)
    dma = pltpu.SemaphoreType.DMA
    hid_p, hid_c, kv = pl.pallas_call(
        kernel,
        out_shape=(
            jax.ShapeDtypeStruct((2, BLK, W), BF16),
            jax.ShapeDtypeStruct((2, CBLK, W), BF16),
            jax.ShapeDtypeStruct((2, 2 * BLK, W), BF16),
        ),
        in_specs=[any_, any_, any_, smem, any_, any_, any_, any_, vmem, vmem, vmem, vmem],
        out_specs=(vmem, vmem, vmem),
        scratch_shapes=[
            pltpu.VMEM((D, W), BF16),
            pltpu.VMEM((D, W), BF16),
            pltpu.VMEM((D, W), BF16),
            pltpu.VMEM((TP, W, W), BF16),
            pltpu.VMEM((TP, 2, BLK, W), BF16),
            pltpu.VMEM((TP, 2, CBLK, W), BF16),
            pltpu.VMEM((ALL, 128), F32),
            pltpu.VMEM((ALL, 128), F32),
            pltpu.VMEM((2, 8, 256), F32),
            pltpu.VMEM((2, TP, 8, 256), F32),
            pltpu.VMEM((ZN, 2, BLK, W), BF16),
            pltpu.VMEM((2, 2, KEYS, W), BF16),
            pltpu.VMEM((CGROUP, CROWS, W), BF16),
            pltpu.VMEM((2, CKEYS, W), BF16),
            pltpu.VMEM((CGROUP, CROWS, MSG), BF16),
            pltpu.VMEM((CGROUP, CROWS, MSG), BF16),
            pltpu.VMEM((ZN, 2, BLK, W), BF16),
            pltpu.VMEM((ZN, 2, BLK, W), BF16),
            pltpu.VMEM((ZN, 8, 128), F32),
            pltpu.VMEM((ZN, 8, 128), F32),
            pltpu.VMEM((2, ZN, 2, 16, W), BF16),
            pltpu.VMEM((2, ZN, 2, 16, W), BF16),
            pltpu.VMEM((ALL, W), BF16),
            pltpu.VMEM((TP, ALL, W), BF16),
            pltpu.VMEM((TP, ALL, W), BF16),
            pltpu.VMEM((8, 128), F32),
            pltpu.VMEM((YN * CN, 8, 128), F32),
            dma((6 + TP,)),
            dma((7,)), dma((TP,)), dma((7,)), dma((TP,)),
            dma((2, 7)), dma((2, TP)),
            dma((3,)), dma((QUAD,)), dma((3,)), dma((QUAD,)),
            pltpu.SemaphoreType.REGULAR,
            dma((CGROUP,)), dma((CGROUP,)),
            dma((ZN,)), dma((ZN,)),
            dma((2, 5, 2, 2)), dma((2, 5, 2, 2)),
            dma((YN, 2, 2)), dma((YN, 2, 2)),
            dma((CGROUP,)), dma((CGROUP,)),
            dma((ZN,)), dma((ZN,)), dma((ZN,)), dma((ZN,)),
            dma((2, ZN)), dma((2, ZN)),
            dma((7,)), dma((TP,)),
            dma((YN * CN,)), dma((YN * CN,)),
        ],
        compiler_params=pltpu.CompilerParams(
            collective_id=0, has_side_effects=True, vmem_limit_bytes=60 * 1024 * 1024
        ),
        name="block",
    )(
        prompt_states[:, 0], cont_states[:, 0], cache_kv[:, 0], cache_lengths,
        w_query, w_key, w_value, w_out,
        q_gain[None], k_gain[None], post_gain[None], inv,
    )
    return hid_p[:, None], hid_c[:, None], kv[:, None]


def solution(mesh):
    return jax.shard_map(
        per_device,
        mesh=mesh,
        in_specs=(
            P(None, "seq", None, "tp"),
            P(None, "seq", None, "tp"),
            P(None, "seq", None, "tp"),
            P(),
            P(None, "tp"),
            P(None, "tp"),
            P(None, "tp"),
            P("tp", None),
            P("tp"),
            P("tp"),
            P("tp"),
        ),
        out_specs=(
            P(None, "seq", None, "tp"),
            P(None, "seq", None, "tp"),
            P(None, "seq", None, "tp"),
        ),
        check_vma=False,
    )
```

```python
import math
import jax
import jax.numpy as jnp
import numpy as np
from jax import lax
from jax.experimental import pallas as pl
from jax.experimental.pallas import tpu as pltpu
from jax.sharding import PartitionSpec as P

HD = 128
EPS = 1e-06
THETA = 500000.0
NEG = -1e30
ZN, YN, CN, TP = 4, 8, 2, 8
BLK, CBLK, CAP = 64, 8, 448
ROWS = 2 * BLK
CROWS = 2 * CBLK
ALL = ROWS + CROWS
W = 256
D = 2048
CACHED = 14336
KEYS = YN * CN * BLK
QUAD = 4
CGROUP = ZN * YN // 2
CKEYS = 1920
MSG = W + 128
QSCALE = math.log2(math.e) / math.sqrt(HD)
F32, BF16 = jnp.float32, jnp.bfloat16


def iota(shape, dim):
    return lax.broadcasted_iota(jnp.int32, shape, dim)


def attend(q, k, v, allowed, k_scale=None):
    s = lax.dot_general(q, k, (((1,), (1,)), ((), ())), preferred_element_type=F32)
    if k_scale is not None:
        s = s * k_scale
    s = jnp.where(allowed, s, NEG)
    m = jnp.max(s, -1, keepdims=True).astype(BF16).astype(F32)
    p = jnp.exp2(s - jnp.maximum(m, -1e29))
    total = jnp.sum(p, -1, keepdims=True)
    out = jnp.dot(p.astype(BF16), v, preferred_element_type=F32)
    return out, m, total


def message(parts):
    rows = parts[0][0].shape[0]
    lane = iota((rows, 128), 1)
    stats = jnp.zeros((rows, 128), F32)
    for h, (_, m, total) in enumerate(parts):
        high = total.astype(BF16).astype(F32)
        stats = jnp.where(lane == 3 * h, m, stats)
        stats = jnp.where(lane == 3 * h + 1, high, stats)
        stats = jnp.where(lane == 3 * h + 2, total - high, stats)
    return jnp.concatenate([p[0].astype(BF16) for p in parts] + [stats.astype(BF16)], -1)


def combine(pieces, stats):
    outs = []
    for h in range(2):
        top = stats[0][h][0]
        for st in stats[1:]:
            top = jnp.maximum(top, st[h][0])
        num, den = 0.0, 0.0
        for p, st in zip(pieces, stats):
            w = jnp.exp2(st[h][0] - top)
            num = num + w * p[:, h * HD : (h + 1) * HD].astype(F32)
            den = den + w * st[h][1]
        outs.append(num / den)
    return jnp.concatenate(outs, -1).astype(BF16)


def message_stats(piece):
    st = piece[:, W:].astype(F32)
    return [
        (st[:, 3 * h : 3 * h + 1], st[:, 3 * h + 1 : 3 * h + 2] + st[:, 3 * h + 2 : 3 * h + 3])
        for h in range(2)
    ]


def kernel(
    prompt, cont, cache, lengths, wq_h, wk_h, wv_h, wo_h, qgain, kgain, pgain, inv,
    hid_p, hid_c, kv_out,
    wq, wk, wv, wo, xg, xc, cos, sin, sq_out, sq_in, qg, kvg, qcg, kcc,
    oc_out, oc_in, op_out, op_in, os_out, os_in, kv_s, kv_r, att, pr_out, pr_in,
    ks_out, ks_in, zr_lo, zr_hi,
    local, tp_ss, tp_rs, tpf_ss, sq_ss, sq_rs, cache_ss, cache_rs, new_ss, new_rs, ready,
    qc_ss, qc_rs, q_ss, q_rs, ring_ss, ring_rs, pair_ss, pair_rs,
    oc_ss, oc_rs, op_ss, op_rs, os_ss, os_rs, kv_ss, kv_rs, pr_ss, pr_rs,
    ks_ss, ks_rs, qf_ss, zr_ss, zr_rs, zf_ss, zf_rs,
):
    s_idx = lax.axis_index("seq")
    t = lax.axis_index("tp")
    z = s_idx // (YN * CN)
    y = (s_idx // CN) % YN
    c = s_idx % CN
    x, zl = t // 2, t % 2

    def seq_of(z_, y_, c_):
        return (z_ * YN + y_) * CN + c_

    def remote(src, dst, ss, rs, seq=None, tp=None):
        dev = {"seq": s_idx if seq is None else seq, "tp": t if tp is None else tp}
        return pltpu.make_async_remote_copy(
            src_ref=src, dst_ref=dst, send_sem=ss, recv_sem=rs,
            device_id=dev, device_id_type=pl.DeviceIdType.MESH,
        )

    partner = s_idx + 1 - 2 * c
    b = y % 2
    slot = 2 * b + c
    base = s_idx - slot
    twin = seq_of(z, y + 1 - 2 * b, c)
    cross = seq_of(z, y + 1 - 2 * b, 1 - c)
    twin_slot = 2 * (1 - b) + c
    group = z * (YN // 2) + y // 2

    def member(i):
        return seq_of(i // (YN // 2), (i % (YN // 2)) * 2 + b, c)

    def cache_rows(j):
        return kcc.at[:, pl.ds(pl.multiple_of(j * CAP, 64), CAP), :]

    def new_rows(j):
        return kcc.at[:, pl.ds(pl.multiple_of(QUAD * CAP + j * CROWS, CROWS), CROWS), :]

    hops = [(0, 1), (1, 0), (3, 0), (1, 1), (3, 1), (2, 0), (2, 1)]
    peers = [((x + dx) % 4) * 2 + (zl + dz) % 2 for dx, dz in hops]

    loads = [
        pltpu.make_async_copy(prompt, xg.at[t], local.at[0]),
        pltpu.make_async_copy(cont, xc.at[t], local.at[1]),
        pltpu.make_async_copy(wq_h, wq, local.at[2]),
        pltpu.make_async_copy(wk_h, wk, local.at[3]),
        pltpu.make_async_copy(wv_h, wv, local.at[4]),
        pltpu.make_async_copy(cache, cache_rows(slot), local.at[5]),
    ] + [
        pltpu.make_async_copy(wo_h.at[:, i * W : (i + 1) * W], wo.at[i], local.at[6 + i])
        for i in range(TP)
    ]
    for load in loads:
        load.start()

    def signal(sem, seq, tp):
        pl.semaphore_signal(
            sem, inc=1, device_id={"seq": seq, "tp": tp}, device_id_type=pl.DeviceIdType.MESH
        )

    barrier = pltpu.get_barrier_semaphore()
    here = 2 * y + c
    greeted = [(s_idx, p) for p in peers]
    greeted += [(z * (YN * CN) + (here + i) % (YN * CN), t) for i in range(1, YN * CN)]
    greeted += [(seq_of((z + i) % ZN, y, c), t) for i in (1, 2, 3)]
    for seq, tp in greeted:
        signal(barrier, seq, tp)

    pl.semaphore_wait(barrier, len(greeted))
    for i in (1, 2, 3):
        signal(ready, seq_of((z + i) % ZN, y, c), t)

    sends = []
    def row_part(i, part, origin, to):
        if origin is None:
            src, origin = (cont if part == 2 else prompt.at[part]), t
        else:
            src = xc.at[origin] if part == 2 else xg.at[origin, part]
        dst = xc.at[origin] if part == 2 else xg.at[origin, part]
        ss = tp_ss.at[i, part] if i < 5 else tpf_ss.at[i - 5, part]
        return remote(src, dst, ss, tp_rs.at[origin, part], tp=to)

    for part in range(3):
        for i in (1, 2, 3, 4, 0):
            d = row_part(i, part, None, peers[i])
            d.start()
            sends.append(d)
    for i, seq in ((0, twin), (1, partner)):
        d = remote(cache, cache_rows(slot), cache_ss.at[i], cache_rs.at[slot], seq=seq)
        d.start()
        sends.append(d)

    r = iota((ALL, 128), 0)
    low_p = s_idx * BLK + r
    high_p = (2 * CN * YN * ZN - 1 - s_idx) * BLK + r - BLK
    low_c = CACHED + s_idx * CBLK + r - ROWS
    high_c = CACHED + (2 * CN * YN * ZN - 1 - s_idx) * CBLK + r - ROWS - CBLK
    pos = jnp.where(
        r < BLK, low_p, jnp.where(r < ROWS, high_p, jnp.where(r < ROWS + CBLK, low_c, high_c))
    )
    angle = pos.astype(F32) * inv[...]
    cos[...] = jnp.cos(angle)
    sine = jnp.sin(angle)
    sin[...] = jnp.where(iota((ALL, 128), 1) < HD // 2, -sine, sine)
    pad0 = QUAD * (CAP + CROWS)
    kcc[:, pad0:, :] = jnp.zeros((2, CKEYS - pad0, W), BF16)

    for load in loads[:5]:
        load.wait()
    qp = jnp.zeros((ALL, W), F32)
    kp = jnp.zeros((ALL, W), F32)
    vp = jnp.zeros((ALL, W), F32)
    for i in (-1, 2, 1, 0, 4, 3, 5, 6):
        if i < 0:
            src = t
        else:
            src = peers[i]
            for part in range(3):
                row_part(0, part, src, src).wait_recv()
                if (i == 2 and part != 1) or (i == 1 and part == 1):
                    for to in range(2):
                        near = ((x + 1) % 4 if i == 2 else (x + 3) % 4) * 2 + to
                        d = row_part(5 + to, part, src, near)
                        d.start()
                        sends.append(d)
        rows = jnp.concatenate(
            [
                xg[src].reshape(ROWS, W),
                xc[src].astype(F32).reshape(CROWS, W).astype(BF16),
            ],
            0,
        )
        ks = pl.ds(pl.multiple_of(src * W, W), W)
        qp += jnp.dot(rows, wq[ks, :], preferred_element_type=F32)
        kp += jnp.dot(rows, wk[ks, :], preferred_element_type=F32)
        vp += jnp.dot(rows, wv[ks, :], preferred_element_type=F32)

    lane = iota((ALL, 128), 1)

    def send_squares(columns, phase):
        stat = jnp.zeros((ALL, 128), F32)
        for j, col in enumerate(columns):
            stat = jnp.where(lane == j, col, stat)
        stat = jnp.concatenate([stat, jnp.zeros((256 - ALL, 128), F32)], 0)
        sq_out[phase] = stat.T[:8, :]
        for i in (6, 5, 4, 3, 2, 1, 0):
            d = remote(
                sq_out.at[phase], sq_in.at[phase, t], sq_ss.at[phase, i], sq_rs.at[phase, t],
                tp=peers[i],
            )
            d.start()
            sends.append(d)

    def total_squares(count, phase):
        total = sq_out[phase]
        for i in range(7):
            remote(
                sq_out.at[phase], sq_in.at[phase, peers[i]], sq_ss.at[phase, i],
                sq_rs.at[phase, peers[i]], tp=peers[i],
            ).wait_recv()
            total = total + sq_in[phase, peers[i]]
        back = jnp.concatenate([total, jnp.zeros((120, 256), F32)], 0).T
        return [back[:ALL, j : j + 1] for j in range(count)]

    send_squares([jnp.sum(qp * qp, -1, keepdims=True), jnp.sum(kp * kp, -1, keepdims=True)], 0)

    own = pl.ds(pl.multiple_of(here * BLK, BLK), BLK)

    def rotate(field):
        outs = []
        for h in range(2):
            f = field[:, h * HD : (h + 1) * HD]
            outs.append(f * cos[...] + pltpu.roll(f, HD // 2, 1) * sin[...])
        return jnp.concatenate(outs, -1)

    def keep(kv, field):
        kvg[kv, 0, own, :] = field[:BLK]
        kvg[kv, 1, own, :] = field[BLK:ROWS]

    def piece(origin_y, core, kv, half):
        rows = pl.ds(pl.multiple_of((2 * origin_y + core) * BLK, BLK), BLK)
        return kvg.at[kv, half, rows, :]

    right, left = seq_of(z, (y + 1) % YN, c), seq_of(z, (y + YN - 1) % YN, c)

    def ring(direction, step, kv, half, origin):
        return remote(
            piece(origin, c, kv, half), piece(origin, c, kv, half),
            ring_ss.at[direction, step, kv, half], ring_rs.at[direction, step, kv, half],
            seq=right if direction == 0 else left,
        )

    def pair(origin, core, kv, half):
        return remote(
            piece(origin, core, kv, half), piece(origin, core, kv, half),
            pair_ss.at[origin, kv, half], pair_rs.at[origin, kv, half], seq=partner,
        )

    def start_pair(origin, kv, half):
        d = pair(origin, c, kv, half)
        d.start()
        sends.append(d)

    def launch(step, kv):
        for half in range(2):
            for direction in range(2):
                origin = (y + (YN - step + 1 if direction == 0 else step - 1)) % YN
                if step > 1:
                    ring(direction, step - 1, kv, half, origin).wait_recv()
                if step < 4 or direction == half:
                    d = ring(direction, step, kv, half, origin)
                    d.start()
                    sends.append(d)
                if step > 1 or direction == 0:
                    start_pair(origin, kv, half)

    def finish(kv):
        for half in range(2):
            far = (y + 4) % YN
            ring(half, 4, kv, half, far).wait_recv()
            start_pair(far, kv, half)

    def wait_pairs(kv):
        for origin in range(YN):
            for half in range(2):
                pair(origin, 1 - c, kv, half).wait_recv()

    values = vp.astype(BF16)
    keep(1, values)
    launch(1, 1)
    turned = rotate(kp * kgain[...])
    keep(0, turned.astype(BF16))
    launch(1, 0)
    launch(2, 1)
    q_sq, k_sq = total_squares(2, 0)
    q_scale = lax.rsqrt(q_sq / D + EPS)
    k_scale = lax.rsqrt(k_sq / D + EPS)
    ks_out[...] = jnp.where(lane[:ROWS] == 0, k_scale[:ROWS], 0.0).T[:8, :]
    new_rows(slot)[0] = (turned[ROWS:] * k_scale[ROWS:]).astype(BF16)
    new_rows(slot)[1] = values[ROWS:]
    queries = (rotate(qp * q_scale * qgain[...]) * QSCALE).astype(BF16)

    def send_scale(i, other):
        return remote(ks_out, ks_in.at[here], ks_ss.at[i], ks_rs.at[here],
                      seq=z * (YN * CN) + other)

    def start_scale(i, carry):
        send_scale(i, (here + i) % (YN * CN)).start()
        return carry

    lax.fori_loop(1, YN * CN, start_scale, 0)
    ks_in[here] = ks_out[...]
    launch(2, 0)
    qcg[group] = queries[ROWS:]
    qg[z] = queries[:ROWS].reshape(2, BLK, W)

    pl.semaphore_wait(ready, 3)

    def cont_q(i, other):
        return remote(qcg.at[group], qcg.at[group], qc_ss.at[i], qc_rs.at[group],
                      seq=member(other))

    def start_cont_q(i, carry):
        cont_q(i, (group + i) % CGROUP).start()
        return carry

    lax.fori_loop(1, CGROUP, start_cont_q, 0)
    for i, seq in ((0, partner), (1, twin), (2, cross)):
        d = remote(new_rows(slot), new_rows(slot), new_ss.at[i], new_rs.at[slot], seq=seq)
        d.start()
        sends.append(d)

    def prompt_q(i, half, origin, dst):
        ss = q_ss.at[i, half] if i < 2 else qf_ss.at[half]
        return remote(qg.at[origin, half], qg.at[origin, half], ss, q_rs.at[origin, half],
                      seq=seq_of(dst, y, c))

    up, down, over = (z + 1) % ZN, (z + 3) % ZN, (z + 2) % ZN
    for half in range(2):
        for i, dst in ((0, up), (1, down)):
            d = prompt_q(i, half, z, dst)
            d.start()
            sends.append(d)

    launch(3, 1)
    remote(cache, cache_rows(twin_slot), cache_ss.at[0], cache_rs.at[twin_slot],
           seq=twin).wait_recv()
    d = remote(cache_rows(twin_slot), cache_rows(twin_slot), cache_ss.at[2],
               cache_rs.at[twin_slot], seq=partner)
    d.start()
    sends.append(d)
    launch(3, 0)
    launch(4, 1)
    launch(4, 0)
    for half, origin, dst in ((0, down, up), (1, up, down)):
        prompt_q(0, half, origin, dst).wait_recv()
        d = prompt_q(2, half, origin, dst)
        d.start()
        sends.append(d)

    loads[5].wait()
    for i, j in ((1, 2 * b + 1 - c), (2, 2 * (1 - b) + 1 - c)):
        remote(cache, cache_rows(j), cache_ss.at[i], cache_rs.at[j], seq=partner).wait_recv()
    for i, j in ((0, 2 * b + 1 - c), (1, twin_slot), (2, 2 * (1 - b) + 1 - c)):
        remote(new_rows(j), new_rows(j), new_ss.at[i], new_rs.at[j], seq=partner).wait_recv()

    def wait_cont_q(i, carry):
        other = (group + i) % CGROUP
        remote(qcg.at[other], qcg.at[other], qc_ss.at[i], qc_rs.at[other],
               seq=member(other)).wait_recv()
        return carry

    lax.fori_loop(1, CGROUP, wait_cont_q, 0)
    top = 2 * CN * YN * ZN - 1
    n = iota((1, CKEYS), 1)
    dead = 1 << 30
    j = n - QUAD * CAP
    key_dev = base + j // CROWS
    in_block = j % CROWS
    new_pos = jnp.where(
        in_block < CBLK,
        key_dev * CBLK + in_block,
        (top - key_dev) * CBLK + in_block - CBLK,
    )
    key_pos = jnp.where((n >= QUAD * CAP) & (n < pad0), new_pos, dead)
    for i in range(QUAD):
        live = (n >= i * CAP) & (n < i * CAP + lengths[base + i])
        key_pos = jnp.where(live, -1, key_pos)

    def cont_block(blk, carry):
        rq = blk * 128 + iota((128, 1), 0)
        who = rq // CROWS
        dev = seq_of(who // (YN // 2), (who % (YN // 2)) * 2 + b, c)
        off = rq % CROWS
        q_pos = jnp.where(off < CBLK, dev * CBLK + off, (top - dev) * CBLK + off - CBLK)
        allowed = key_pos <= q_pos
        q = qcg[pl.ds(blk * 8, 8)].reshape(128, W)
        parts = [
            attend(
                q[:, h * HD : (h + 1) * HD],
                kcc[0, :, h * HD : (h + 1) * HD],
                kcc[1, :, h * HD : (h + 1) * HD],
                allowed,
            )
            for h in range(2)
        ]
        oc_out[pl.ds(blk * 8, 8)] = message(parts).reshape(8, CROWS, MSG)
        return carry

    cont_block(0, 0)
    finish(1)
    cont_block(1, 0)

    def cont_o(i, other):
        return remote(oc_out.at[other], oc_in.at[group], oc_ss.at[i], oc_rs.at[group],
                      seq=member(other))

    def start_cont_o(i, carry):
        cont_o(i, (group + i) % CGROUP).start()
        return carry

    lax.fori_loop(1, CGROUP, start_cont_o, 0)

    ro = iota((128, 2 * KEYS), 0)
    co = iota((128, 2 * KEYS), 1)
    jj = ro % 16
    want = (ro // 32) * 16 + here
    pick_row = jnp.where(ro % 32 < 16, jj * BLK, KEYS + (15 - jj) * BLK) + want
    onehot = jnp.where(co == pick_row, 1.0, 0.0).astype(BF16)

    def cyclic_rows(kv):
        rows = jnp.dot(onehot, kvg[kv].reshape(2 * KEYS, W), preferred_element_type=F32)
        if kv == 0:
            rows = rows * jnp.sum(jnp.where(co == pick_row, key_scale, 0.0), -1, keepdims=True)
        kv_s[kv] = rows.astype(BF16).reshape(ZN, 2, 16, W)
        for i in (2, 1, 3):
            dst = (z + i) % ZN
            d = remote(kv_s.at[kv, dst], kv_r.at[kv, z], kv_ss.at[kv, i], kv_rs.at[kv, z],
                       seq=seq_of(dst, y, c))
            d.start()
            sends.append(d)

    finish(0)
    wait_pairs(1)
    for half, origin in ((1, down), (0, up), (0, over), (1, over)):
        prompt_q(0, half, origin, origin).wait_recv()

    def wait_scale(i, carry):
        other = (here + i) % (YN * CN)
        remote(ks_out, ks_in.at[other], ks_ss.at[i], ks_rs.at[other],
               seq=z * (YN * CN) + other).wait_recv()
        return carry

    lax.fori_loop(1, YN * CN, wait_scale, 0)
    low_half = iota((8, 128), 1) < BLK
    lows, highs = [], []
    for i in range(YN):
        first, second = ks_in[2 * i], ks_in[2 * i + 1]
        lows.append(jnp.where(low_half, first, pltpu.roll(second, BLK, 1))[:1])
        highs.append(jnp.where(low_half, pltpu.roll(first, BLK, 1), second)[:1])
    key_scale = jnp.concatenate(lows + highs, 1)
    wait_pairs(0)

    n2 = iota((1, 2 * KEYS), 1)
    hi_n = n2 - KEYS
    key_pos2 = jnp.where(
        n2 < KEYS,
        z * KEYS + n2,
        (top - z * (YN * CN) - hi_n // BLK) * BLK + hi_n % BLK,
    )

    def prompt_block(i, carry):
        zq = (z + i) % ZN
        dev = zq * (YN * CN) + here
        rq = iota((ROWS, 1), 0)
        q_pos = jnp.where(rq < BLK, dev * BLK + rq, (top - dev) * BLK + rq - BLK)
        allowed = key_pos2 <= q_pos
        q = qg[zq].reshape(ROWS, W)
        parts = [
            attend(
                q[:, h * HD : (h + 1) * HD],
                kvg[0, :, :, h * HD : (h + 1) * HD].reshape(2 * KEYS, HD),
                kvg[1, :, :, h * HD : (h + 1) * HD].reshape(2 * KEYS, HD),
                allowed,
                key_scale,
            )
            for h in range(2)
        ]
        op_out[zq] = jnp.concatenate([p[0].astype(BF16) for p in parts], -1).reshape(2, BLK, W)
        stats = jnp.zeros((ROWS, 128), F32)
        for h in range(2):
            stats = jnp.where(lane[:ROWS] == 2 * h, parts[h][1], stats)
            stats = jnp.where(lane[:ROWS] == 2 * h + 1, parts[h][2], stats)
        os_out[zq] = stats.T[:8, :]
        return carry

    def stats_o(i, dst):
        return remote(os_out.at[dst], os_in.at[z], os_ss.at[i], os_rs.at[z],
                      seq=seq_of(dst, y, c))

    def near_o(i, dst):
        return remote(op_out.at[dst], op_in.at[z], op_ss.at[i], op_rs.at[z],
                      seq=seq_of(dst, y, c))

    def far_o(half, dst):
        return remote(op_out.at[over, half], zr_lo if half == 0 else zr_hi, zr_ss.at[half],
                      zr_rs.at[half], seq=seq_of(dst, y, c))

    def pass_o(half, origin, dst):
        return remote(zr_lo if half == 0 else zr_hi, op_in.at[origin, half], zf_ss.at[half],
                      zf_rs.at[half], seq=seq_of(dst, y, c))

    def go(*copies):
        for d in copies:
            d.start()
            sends.append(d)

    prompt_block(2, 0)
    go(far_o(0, up), far_o(1, down), stats_o(2, over))
    prompt_block(1, 0)
    go(near_o(1, up), stats_o(1, up))
    prompt_block(3, 0)
    go(near_o(3, down), stats_o(3, down))
    far_o(0, up).wait_recv()
    go(pass_o(0, down, up))
    far_o(1, down).wait_recv()
    go(pass_o(1, up, down))
    prompt_block(0, 0)

    def wait_cont_o(i, carry):
        other = (group + i) % CGROUP
        remote(oc_out.at[other], oc_in.at[other], oc_ss.at[i], oc_rs.at[other],
               seq=member(other)).wait_recv()
        return carry

    lax.fori_loop(1, CGROUP, wait_cont_o, 0)
    oc_in[group] = oc_out[group]
    cont_parts = [oc_in[i] for i in range(CGROUP)]
    att[ROWS:, :] = combine(cont_parts, [message_stats(p) for p in cont_parts])
    pieces, stats = [op_out[z].reshape(ROWS, W)], [os_out[z]]
    for i in (1, 3, 2):
        src = (z + i) % ZN
        if i == 2:
            pass_o(0, src, z).wait_recv()
            pass_o(1, src, z).wait_recv()
        else:
            remote(op_out.at[src], op_in.at[src], op_ss.at[i], op_rs.at[src],
                   seq=seq_of(src, y, c)).wait_recv()
        remote(os_out.at[src], os_in.at[src], os_ss.at[i], os_rs.at[src],
               seq=seq_of(src, y, c)).wait_recv()
        pieces.append(op_in[src].reshape(ROWS, W))
        stats.append(os_in[src])
    cols = jnp.concatenate(stats + [jnp.zeros((96, 128), F32)], 0).T
    att[:ROWS, :] = combine(
        pieces,
        [
            [
                (cols[:, 8 * i + 2 * h : 8 * i + 2 * h + 1],
                 cols[:, 8 * i + 2 * h + 1 : 8 * i + 2 * h + 2])
                for h in range(2)
            ]
            for i in range(ZN)
        ],
    )

    for load in loads[6:]:
        load.wait()
    a = att[...]

    def project(p):
        return jnp.dot(a, wo[p], preferred_element_type=F32).astype(BF16)

    for i in (6, 5, 4, 3, 2, 1, 0):
        p = peers[i]
        pr_out[p] = project(p)
        go(remote(pr_out.at[p], pr_in.at[t], pr_ss.at[i], pr_rs.at[t], tp=p))
    cyclic_rows(1)
    cyclic_rows(0)
    proj = project(t).astype(F32)
    for i in range(7):
        p = peers[i]
        remote(pr_out.at[p], pr_in.at[p], pr_ss.at[i], pr_rs.at[p], tp=p).wait_recv()
        proj = proj + pr_in[p].astype(F32)

    send_squares([jnp.sum(proj * proj, -1, keepdims=True)], 1)
    (p_sq,) = total_squares(1, 1)
    normed = proj * lax.rsqrt(p_sq / D + EPS) * pgain[...]
    hid_p[...] = (xg[t].astype(F32) + normed[:ROWS].reshape(2, BLK, W)).astype(BF16)
    hid_c[...] = (xc[t].astype(F32) + normed[ROWS:].reshape(2, CBLK, W)).astype(BF16)

    for kv in range(2):
        for i in (1, 3, 2):
            src = (z + i) % ZN
            remote(kv_s.at[kv, src], kv_r.at[kv, src], kv_ss.at[kv, i], kv_rs.at[kv, src],
                   seq=seq_of(src, y, c)).wait_recv()
        kv_r[kv, z] = kv_s[kv, z]
        for src in range(ZN):
            kv_out[kv, 16 * src : 16 * src + 16, :] = kv_r[kv, src, 0]
            kv_out[kv, 112 - 16 * src : 128 - 16 * src, :] = kv_r[kv, src, 1]

    for d in sends:
        d.wait_send()

    def drain(i, carry):
        cont_q(i, (group + i) % CGROUP).wait_send()
        cont_o(i, (group + i) % CGROUP).wait_send()
        send_scale(i, (here + i) % (YN * CN)).wait_send()
        return carry

    lax.fori_loop(1, CGROUP, drain, 0)


def per_device(
    prompt_states, cont_states, cache_kv, cache_lengths, w_query, w_key, w_value, w_out,
    q_gain, k_gain, post_gain,
):
    half = HD // 2
    freq = THETA ** (-(np.arange(half) * 2.0 / HD))
    inv = jnp.asarray(np.concatenate([freq, freq])[None, :].astype(np.float32))
    any_ = pl.BlockSpec(memory_space=pl.ANY)
    vmem = pl.BlockSpec(memory_space=pltpu.VMEM)
    smem = pl.BlockSpec(memory_space=pltpu.SMEM)
    dma = pltpu.SemaphoreType.DMA
    hid_p, hid_c, kv = pl.pallas_call(
        kernel,
        out_shape=(
            jax.ShapeDtypeStruct((2, BLK, W), BF16),
            jax.ShapeDtypeStruct((2, CBLK, W), BF16),
            jax.ShapeDtypeStruct((2, 2 * BLK, W), BF16),
        ),
        in_specs=[any_, any_, any_, smem, any_, any_, any_, any_, vmem, vmem, vmem, vmem],
        out_specs=(vmem, vmem, vmem),
        scratch_shapes=[
            pltpu.VMEM((D, W), BF16),
            pltpu.VMEM((D, W), BF16),
            pltpu.VMEM((D, W), BF16),
            pltpu.VMEM((TP, W, W), BF16),
            pltpu.VMEM((TP, 2, BLK, W), BF16),
            pltpu.VMEM((TP, 2, CBLK, W), BF16),
            pltpu.VMEM((ALL, 128), F32),
            pltpu.VMEM((ALL, 128), F32),
            pltpu.VMEM((2, 8, 256), F32),
            pltpu.VMEM((2, TP, 8, 256), F32),
            pltpu.VMEM((ZN, 2, BLK, W), BF16),
            pltpu.VMEM((2, 2, KEYS, W), BF16),
            pltpu.VMEM((CGROUP, CROWS, W), BF16),
            pltpu.VMEM((2, CKEYS, W), BF16),
            pltpu.VMEM((CGROUP, CROWS, MSG), BF16),
            pltpu.VMEM((CGROUP, CROWS, MSG), BF16),
            pltpu.VMEM((ZN, 2, BLK, W), BF16),
            pltpu.VMEM((ZN, 2, BLK, W), BF16),
            pltpu.VMEM((ZN, 8, 128), F32),
            pltpu.VMEM((ZN, 8, 128), F32),
            pltpu.VMEM((2, ZN, 2, 16, W), BF16),
            pltpu.VMEM((2, ZN, 2, 16, W), BF16),
            pltpu.VMEM((ALL, W), BF16),
            pltpu.VMEM((TP, ALL, W), BF16),
            pltpu.VMEM((TP, ALL, W), BF16),
            pltpu.VMEM((8, 128), F32),
            pltpu.VMEM((YN * CN, 8, 128), F32),
            pltpu.VMEM((BLK, W), BF16),
            pltpu.VMEM((BLK, W), BF16),
            dma((6 + TP,)),
            dma((5, 3)), dma((TP, 3)), dma((2, 3)),
            dma((2, 7)), dma((2, TP)),
            dma((3,)), dma((QUAD,)), dma((3,)), dma((QUAD,)),
            pltpu.SemaphoreType.REGULAR,
            dma((CGROUP,)), dma((CGROUP,)),
            dma((2, 2)), dma((ZN, 2)),
            dma((2, 5, 2, 2)), dma((2, 5, 2, 2)),
            dma((YN, 2, 2)), dma((YN, 2, 2)),
            dma((CGROUP,)), dma((CGROUP,)),
            dma((ZN,)), dma((ZN,)), dma((ZN,)), dma((ZN,)),
            dma((2, ZN)), dma((2, ZN)),
            dma((7,)), dma((TP,)),
            dma((YN * CN,)), dma((YN * CN,)), dma((2,)),
            dma((2,)), dma((2,)), dma((2,)), dma((2,)),
        ],
        compiler_params=pltpu.CompilerParams(
            collective_id=0, has_side_effects=True, vmem_limit_bytes=60 * 1024 * 1024
        ),
        name="block",
    )(
        prompt_states[:, 0], cont_states[:, 0], cache_kv[:, 0], cache_lengths,
        w_query, w_key, w_value, w_out,
        q_gain[None], k_gain[None], post_gain[None], inv,
    )
    return hid_p[:, None], hid_c[:, None], kv[:, None]


def solution(mesh):
    return jax.shard_map(
        per_device,
        mesh=mesh,
        in_specs=(
            P(None, "seq", None, "tp"),
            P(None, "seq", None, "tp"),
            P(None, "seq", None, "tp"),
            P(),
            P(None, "tp"),
            P(None, "tp"),
            P(None, "tp"),
            P("tp", None),
            P("tp"),
            P("tp"),
            P("tp"),
        ),
        out_specs=(
            P(None, "seq", None, "tp"),
            P(None, "seq", None, "tp"),
            P(None, "seq", None, "tp"),
        ),
        check_vma=False,
    )
```
